256 devices in a mesh: row: 8 (over y, x_lo), col: 32 (over x_hi, z, core).
Axes of the slice: x: 4 (x_hi: 2, x_lo: 2; x = x_hi * 2 + x_lo), y: 4, z: 8, core: 2. Of those that a mesh axis runs over, the one named last changes fastest.
Arguments:
- features: bfloat16 [32768, 768], P(('row', 'col')), may hold values from -6 to 6
- cotangent: bfloat16 [32768, 768], P(('row', 'col')), may hold values from -6 to 6
- w_self: bfloat16 [768, 768], replicated, may hold values from -0.21875 to 0.21875
- w_neigh: bfloat16 [768, 768], replicated, may hold values from -0.21875 to 0.21875
- degree: int32 [32768], P(('row', 'col')), may hold values from 16 to 64
- block_cols: int32 [8, 32, 32, 4], P('row', 'col'), may hold values from 0 to 7, as said below
- block_count: int32 [8, 32, 32], P('row', 'col'), may hold values from 0 to 4, as said below
- blocks: bfloat16 [8, 32, 32, 4, 128, 128], P('row', 'col'), may hold values from 0 to 1, as said below
Outputs:
- output: bfloat16 [32768, 768], P(('row', 'col'))
- grad_features: bfloat16 [32768, 768], P(('row', 'col'))
- grad_w_self: float32 [768, 768], replicated
- grad_w_neigh: float32 [768, 768], replicated
The draws below stay inside these ranges and needn't reach their ends.
Inputs may be any that keep to these rules, and one draw needn't show every extreme that they name: `block_cols`: within one block row of a tile the 4 block columns are distinct. The live slots of a block row are its first block_count ones. `blocks`: every entry of a slot at or past its block row's live count is zero.
All inputs are finite; a program needn't handle non-finite values.
Results may differ from the reference program's by a relative error of at most 0.015.
Values may be sent and summed in bfloat16 or wider, within the bound.
No kernel may reach another device: no remote copies, remote signals or barrier semaphores. Data moves between devices by JAX's collectives and lax.ppermute only.
A program may use at most 128 MiB of HBM per device.

```python
import jax
import jax.numpy as jnp
from jax import lax

D = 768
BLK = 128
SLOTS = 4
NODE_DEV = 128
GRID_R = 8
GRID_C = 32
NODES = 32768
TROWS = 32
SBLK = 8


def tile_loads(key):
    levels = jax.random.randint(jax.random.fold_in(key, 21), (GRID_R, GRID_C, 1), 1, SLOTS + 1)
    levels = levels.at[0, 0, 0].set(SLOTS)
    dropped = jax.random.randint(jax.random.fold_in(key, 22), (GRID_R, GRID_C, TROWS), 0, 2)
    counts = jnp.maximum(levels - dropped, 0)
    counts = counts.at[:, :, 0].set(levels[:, :, 0])
    counts = counts.at[GRID_R - 1, GRID_C - 1, 1].set(0)
    return counts.astype(jnp.int32)


def draw_block_count(key, part):
    return tile_loads(key)


def draw_block_cols(key, part):
    scores = jax.random.randint(jax.random.fold_in(key, 11), (GRID_R, GRID_C, TROWS, SBLK), 0, 1 << 20)
    scores = scores * SBLK + jnp.arange(SBLK, dtype=jnp.int32)
    ranking = jnp.argsort(scores, axis=-1)[..., :SLOTS].astype(jnp.int32)
    ranking = ranking.at[0, 0, 0].set(jnp.arange(SBLK - SLOTS, SBLK, dtype=jnp.int32))
    ranking = ranking.at[0, 0, 1].set(jnp.arange(SLOTS, dtype=jnp.int32))
    return ranking


def draw_blocks(key, part):
    counts = tile_loads(key)
    block_shape = (GRID_R, GRID_C, TROWS, SLOTS, BLK, BLK)
    values_drawn = jax.random.uniform(jax.random.fold_in(key, 31), block_shape, jnp.float32, 0.2, 1.0)
    kept_mask = jax.random.bernoulli(jax.random.fold_in(key, 32), 0.25, block_shape)
    live_mask = jnp.arange(SLOTS, dtype=jnp.int32)[None, None, None, :] < counts[..., None]
    return jnp.where(kept_mask & live_mask[..., None, None], values_drawn, 0.0).astype(jnp.bfloat16)


def with_ends(result, rng, low, top_value):
    extent = result.shape
    place = [jax.random.randint(jax.random.fold_in(rng, axis), (), 0, extent[axis]) for axis in range(len(extent))]
    result = result.at[tuple(place)].set(low)
    longest = extent.index(max(extent))
    place[longest] = (place[longest] + 1) % extent[longest]
    return result.at[tuple(place)].set(top_value)


def level_of(own_key, extent, shards, smallest, high):
    def one(position, blocks):
        heights = jax.random.uniform(jax.random.fold_in(jax.random.fold_in(own_key, 6), position), (blocks,), jnp.float32, smallest / len(shards), high / len(shards))
        return jnp.repeat(jnp.exp(heights), extent[position] // blocks).reshape((-1,) + (1,) * (len(extent) - position - 1))

    loudness = one(*shards[0])
    for cut in shards[1:]:
        loudness = loudness * one(*cut)
    return loudness


def bell_draw(rng, dims, scale, bound, shards=(), held_as=jnp.bfloat16):
    result = scale * jax.random.normal(rng, dims, jnp.float32)
    if shards:
        result = result * level_of(rng, dims, shards, -0.22, 0.18)
    return jnp.clip(result, -bound, bound).astype(held_as)


def setup_inputs(seed: int = 0) -> dict:
    splits = jax.random.split(jax.random.key(seed), 9)
    features = bell_draw(splits[0], (NODES, D), 1.0, 6.0, ((0, 256),))
    cotangent = bell_draw(splits[1], (NODES, D), 1.0, 6.0, ((0, 256),))
    w_self = bell_draw(splits[2], (D, D), D ** -0.5, 0.21875)
    w_neigh = bell_draw(splits[3], (D, D), D ** -0.5, 0.21875)
    degree = with_ends(jax.random.randint(splits[4], (NODES,), 16, 65), jax.random.fold_in(splits[4], 1), 16, 64).astype(jnp.int32)
    block_cols = draw_block_cols(jax.random.fold_in(splits[8], 71), 0)
    block_count = draw_block_count(jax.random.fold_in(splits[8], 71), 0)
    blocks = draw_blocks(jax.random.fold_in(splits[8], 71), 0)
    return {"features": features, "cotangent": cotangent, "w_self": w_self, "w_neigh": w_neigh, "degree": degree, "block_cols": block_cols, "block_count": block_count, "blocks": blocks}


def silu_slope(hidden):
    sigmoid_value = jax.nn.sigmoid(hidden)
    return sigmoid_value * (1.0 + hidden * (1.0 - sigmoid_value))


def live_weights(blocks, block_count, column):
    weights = lax.dynamic_index_in_dim(blocks, column, 1, keepdims=False).astype(jnp.float32)
    counts = lax.dynamic_index_in_dim(block_count, column, 1, keepdims=False)
    live = (jnp.arange(SLOTS, dtype=jnp.int32)[None, None, :] < counts[:, :, None]).astype(jnp.float32)
    return weights * live[:, :, :, None, None]


def reference(features, cotangent, w_self, w_neigh, degree, block_cols, block_count, blocks):
    by_tile = features.reshape(GRID_R, GRID_C, NODE_DEV, D)
    columns = jnp.arange(GRID_C, dtype=jnp.int32)

    def forward_column(running, column):
        sources = lax.dynamic_index_in_dim(by_tile, column, 1, keepdims=False).reshape(SBLK, BLK, D)
        chosen = lax.dynamic_index_in_dim(block_cols, column, 1, keepdims=False)
        weights = live_weights(blocks, block_count, column)
        picked = jnp.take(sources, chosen, axis=0).astype(jnp.float32)
        term = jnp.einsum("itkab,itkbd->itad", weights, picked)
        return running + term, jnp.zeros((), jnp.float32)

    start_sums = jnp.zeros((GRID_R, TROWS, BLK, D), jnp.float32)
    summed, unused = lax.scan(forward_column, start_sums, columns)
    summed = summed.reshape(NODES, D)
    degree_f = degree.astype(jnp.float32)[:, None]
    aggregate = (summed / degree_f).astype(jnp.bfloat16)
    hidden = jnp.dot(features, w_self, preferred_element_type=jnp.float32) + jnp.dot(aggregate, w_neigh, preferred_element_type=jnp.float32)
    output = jax.nn.silu(hidden).astype(jnp.bfloat16)
    hidden_grad = (cotangent.astype(jnp.float32) * silu_slope(hidden)).astype(jnp.bfloat16)
    grad_scale = NODES ** -0.5
    grad_w_self = jnp.dot(features.T, hidden_grad, preferred_element_type=jnp.float32) * grad_scale
    grad_w_neigh = jnp.dot(aggregate.T, hidden_grad, preferred_element_type=jnp.float32) * grad_scale
    neigh_grad = (jnp.dot(hidden_grad, w_neigh.T, preferred_element_type=jnp.float32) / degree_f).astype(jnp.bfloat16)
    targets = neigh_grad.reshape(GRID_R, TROWS, BLK, D).astype(jnp.float32)

    def backward_column(running, column):
        chosen = lax.dynamic_index_in_dim(block_cols, column, 1, keepdims=False)
        weights = live_weights(blocks, block_count, column)
        spread = jnp.einsum("itkab,itad->itkbd", weights, targets)
        placed = jnp.zeros((SBLK, BLK, D), jnp.float32).at[chosen.reshape(-1)].add(spread.reshape(-1, BLK, D))
        return running, placed.reshape(GRID_R, NODE_DEV, D)

    unused_total, back = lax.scan(backward_column, jnp.zeros((), jnp.float32), columns)
    back = back.transpose(1, 0, 2, 3).reshape(NODES, D)
    grad_features = (jnp.dot(hidden_grad, w_self.T, preferred_element_type=jnp.float32) + back).astype(jnp.bfloat16)
    return (output, grad_features, grad_w_self, grad_w_neigh)
```

```python
import functools

import jax
import jax.numpy as jnp
from jax import lax
from jax.experimental import pallas as pl
from jax.experimental.pallas import tpu as pltpu
from jax.sharding import PartitionSpec as P

ROWS, COLS, RING = 8, 32, 8
OFFSETS = (4, 3, 5, 2, 6, 1, 7, 0)
F32, BF16 = jnp.float32, jnp.bfloat16


def to_partner(value):
    return lax.ppermute(value, "col", [(j, j ^ 1) for j in range(COLS)])


def to_far(value):
    return lax.ppermute(value, "col", [(j, j ^ 16) for j in range(COLS)])


def along(value, step):
    pairs = [(j, (j & 17) | (((j // 2 + step) % RING) * 2)) for j in range(COLS)]
    return lax.ppermute(value, "col", pairs)


def to_row(value, flip):
    return lax.ppermute(value, "row", [(i, i ^ flip) for i in range(ROWS)])


def column_groups():
    return [[c for c in range(COLS) if c % 2 == k] for k in range(2)]


def place_kernel(table, cols, count, blocks, dense):
    step = pl.program_id(0)
    dense[...] = jnp.zeros_like(dense)
    for part in range(2):
        row = table[step * 2 + part]
        for slot in range(4):
            @pl.when(slot < count[row])
            def _():
                at = pl.multiple_of(cols[row * 4 + slot] * 128, 128)
                dense[0, part * 128 : part * 128 + 128, pl.ds(at, 128)] = blocks[part][slot]


def place(table, cols, count, blocks):
    def body(table_ref, cols_ref, count_ref, first, second, dense):
        place_kernel(table_ref, cols_ref, count_ref, (first.at[0], second.at[0]), dense)

    spec = [
        pl.BlockSpec((1, 4, 128, 128), functools.partial(lambda part, s, t, c, n: (t[s * 2 + part], 0, 0, 0), part))
        for part in range(2)
    ]
    return pl.pallas_call(
        body,
        out_shape=jax.ShapeDtypeStruct((16, 256, 1024), BF16),
        grid_spec=pltpu.PrefetchScalarGridSpec(
            num_scalar_prefetch=3,
            grid=(16,),
            in_specs=spec,
            out_specs=pl.BlockSpec((1, 256, 1024), lambda s, t, c, n: (s, 0, 0)),
        ),
        compiler_params=pltpu.CompilerParams(vmem_limit_bytes=24 << 20),
    )(table, cols, count, blocks, blocks)


def weight_kernel(table, own, summed, *refs):
    out = refs[-1]
    total = jnp.zeros(out.shape, F32)
    for k, grads in enumerate(refs[:-1]):
        at = table[k]
        left = jnp.concatenate([own[at], summed[at]], axis=0)
        total += jnp.dot(left, grads[...], preferred_element_type=F32)
    out[...] = total


def weight_slices(table, own, summed, grads):
    whole = [pl.BlockSpec(memory_space=pltpu.VMEM)] * (2 + len(grads))
    return pl.pallas_call(
        weight_kernel,
        out_shape=jax.ShapeDtypeStruct((96, 768), F32),
        in_specs=[pl.BlockSpec(memory_space=pltpu.SMEM)] + whole,
        out_specs=pl.BlockSpec(memory_space=pltpu.VMEM),
        compiler_params=pltpu.CompilerParams(vmem_limit_bytes=24 << 20),
    )(table, own, summed, *grads)


def silu_slope(hidden):
    sigmoid_value = jax.nn.sigmoid(hidden)
    return sigmoid_value * (1.0 + hidden * (1.0 - sigmoid_value))


def dot(a, b):
    return jnp.dot(a, b, preferred_element_type=F32)


def per_device(features, cotangent, w_self, w_neigh, degree, block_cols, block_count, blocks):
    row, col = lax.axis_index("row"), lax.axis_index("col")
    core, ring, far = col % 2, (col // 2) % RING, col // 16
    offsets = jnp.array(OFFSETS, jnp.int32)
    ring_at = (ring + offsets) % RING
    core_at = jnp.arange(2, dtype=jnp.int32) ^ core
    far_at = jnp.arange(2, dtype=jnp.int32) ^ far
    table = (
        far_at[None, None, :] * 16 + ring_at[None, :, None] * 2 + core_at[:, None, None]
    ).reshape(-1)
    group_at = (far_at[None, :] * RING + ring_at[:, None]).reshape(-1)
    dense = place(table, (block_cols[0, 0] ^ row).reshape(-1), block_count[0, 0], blocks[0, 0])
    dense = dense.reshape(2, RING, 256, 1024)

    degree_f = degree.astype(F32)[:, None]
    pieces = [features] + [to_row(features, d) for d in range(1, ROWS)]
    sources = jnp.concatenate(pieces, axis=0)
    own_t = (features.astype(F32) * degree_f).astype(BF16).T
    own_slices = lax.all_to_all(
        own_t.reshape(16, 48, 128), "col", 0, 0, axis_index_groups=column_groups(), tiled=True
    )
    self_part = dot(features, w_self)

    groups = ((0, 1), (1, 3), (3, 5), (5, 8))
    crossed = {}
    for lo, hi in groups:
        sent = dot(dense[1, lo:hi].reshape(-1, 1024), sources).astype(BF16)
        got = to_partner(sent)
        for k in range(lo, hi):
            crossed[OFFSETS[k]] = got[(k - lo) * 256 : (k - lo + 1) * 256]
    mine = {}
    for lo, hi in groups:
        kept = dot(dense[0, lo:hi].reshape(-1, 1024), sources)
        for k in range(lo, hi):
            mine[OFFSETS[k]] = kept[(k - lo) * 256 : (k - lo + 1) * 256] + crossed[OFFSETS[k]].astype(F32)

    def half(offset, side):
        return mine[offset % RING][side * 128 : side * 128 + 128]

    arrived = {}
    for reach in (4, 3, 2, 1):
        for step in (1, -1):
            for side in (0, 1):
                if reach == 4 and (side == 0) != (step == 1):
                    continue
                value = half(step * reach, side)
                if (step, side) in arrived:
                    value = value + arrived[step, side].astype(F32)
                arrived[step, side] = along(value.astype(BF16), step)
    ends = [half(0, s) + arrived[1, s].astype(F32) + arrived[-1, s].astype(F32) for s in range(2)]
    summed = ends[0] + to_far(ends[1].astype(BF16)).astype(F32)

    aggregate = (summed / degree_f).astype(BF16)
    hidden = self_part + dot(aggregate, w_neigh)
    output = jax.nn.silu(hidden).astype(BF16)
    slope = cotangent.astype(F32) * silu_slope(hidden)
    hidden_grad = slope.astype(BF16)
    shared = (slope / degree_f).astype(BF16)

    far_shared = to_far(shared)
    held = {(0, 0): shared, (0, 1): far_shared}
    for reach in (1, 2, 3, 4):
        for step in (1, -1):
            for side in (0, 1):
                if reach == 4 and (side == 0) != (step == 1):
                    continue
                held[(-step * reach) % RING, side] = along(held[(-step * (reach - 1)) % RING, side], step)
    summed_slices = lax.all_to_all(
        summed.astype(BF16).T.reshape(16, 48, 128), "col", 0, 0, axis_index_groups=column_groups(), tiled=True
    )
    across = (((0,), (0,)), ((), ()))
    spread = None
    for lo, hi in ((7, 8), (5, 7), (3, 5), (1, 3), (0, 1)):
        here = jnp.concatenate([held[OFFSETS[k], s] for k in range(lo, hi) for s in range(2)], axis=0)
        there = to_partner(here)
        for side, value in ((0, here), (1, there)):
            term = lax.dot_general(
                dense[side, lo:hi].reshape(-1, 1024), value, across, preferred_element_type=F32
            )
            spread = term if spread is None else spread + term
    back = spread[:128]
    for d in range(1, ROWS):
        back = back + to_row(spread[d * 128 : d * 128 + 128].astype(BF16), d).astype(F32)
    against = (((1,), (1,)), ((), ()))
    grad_features = (
        lax.dot_general(hidden_grad, w_self, against, preferred_element_type=F32)
        + lax.dot_general(back.astype(BF16), w_neigh, against, preferred_element_type=F32)
    ).astype(BF16)

    slices = weight_slices(
        group_at, own_slices, summed_slices, [held[o, s] for o in OFFSETS for s in range(2)]
    )
    slices = slices.reshape(2, 48, 768)
    kept = lax.dynamic_index_in_dim(slices, core, 0, keepdims=False)
    sent = lax.dynamic_index_in_dim(slices, 1 - core, 0, keepdims=False)
    pair = (kept + to_partner(sent)).astype(BF16)
    rows_all = lax.all_to_all(
        jnp.broadcast_to(pair[None], (ROWS, 48, 768)), "row", 0, 0, tiled=True
    )
    grad_scale = float(128 * ROWS * COLS) ** (-0.5)
    total = (jnp.sum(rows_all.astype(F32), axis=0) * grad_scale).astype(BF16)
    full = lax.all_to_all(
        jnp.broadcast_to(total[None], (16, 48, 768)), "col", 0, 0, axis_index_groups=column_groups(), tiled=True
    ).reshape(768, 768)
    other = to_partner(full)
    grad_w_self = jnp.where(core == 0, full, other).astype(F32)
    grad_w_neigh = jnp.where(core == 0, other, full).astype(F32)
    return (output, grad_features, grad_w_self, grad_w_neigh)


def solution(mesh):
    placed = (
        P(("row", "col"), None),
        P(("row", "col"), None),
        P(),
        P(),
        P(("row", "col")),
        P("row", "col", None, None),
        P("row", "col", None),
        P("row", "col", None, None, None, None),
    )
    return jax.shard_map(
        per_device,
        mesh=mesh,
        in_specs=placed,
        out_specs=(P(("row", "col"), None), P(("row", "col"), None), P(), P()),
        check_vma=False,
    )
```

```python
import functools

import jax
import jax.numpy as jnp
from jax import lax
from jax.experimental import pallas as pl
from jax.experimental.pallas import tpu as pltpu
from jax.sharding import PartitionSpec as P

ROWS, COLS, RING = 8, 32, 8
OFFSETS = (4, 3, 5, 2, 6, 1, 7, 0)
F32, BF16 = jnp.float32, jnp.bfloat16


def to_partner(value):
    return lax.ppermute(value, "col", [(j, j ^ 1) for j in range(COLS)])


def to_far(value):
    return lax.ppermute(value, "col", [(j, j ^ 16) for j in range(COLS)])


def along(value, step):
    pairs = [(j, (j & 17) | (((j // 2 + step) % RING) * 2)) for j in range(COLS)]
    return lax.ppermute(value, "col", pairs)


def to_row(value, flip):
    return lax.ppermute(value, "row", [(i, i ^ flip) for i in range(ROWS)])


def column_groups():
    return [[c for c in range(COLS) if c % 2 == k] for k in range(2)]


def place_kernel(table, cols, count, first, second, dense, turned):
    step = pl.program_id(0)
    dense[...] = jnp.zeros_like(dense)
    turned[...] = jnp.zeros_like(turned)
    for part, blocks in enumerate((first, second)):
        row = table[step * 2 + part]
        lanes = slice(part * 128, part * 128 + 128)
        for slot in range(4):
            @pl.when(slot < count[row])
            def _():
                at = pl.multiple_of(cols[row * 4 + slot] * 128, 128)
                dense[0, lanes, pl.ds(at, 128)] = blocks[0, slot]
                turned[pl.ds(at, 128), lanes] = blocks[0, slot].T


def place(table, cols, count, blocks):
    def spec(part):
        return pl.BlockSpec((1, 4, 128, 128), lambda s, t, c, n: (t[s * 2 + part], 0, 0, 0))

    return pl.pallas_call(
        place_kernel,
        out_shape=(
            jax.ShapeDtypeStruct((16, 256, 1024), BF16),
            jax.ShapeDtypeStruct((1024, 4096), BF16),
        ),
        grid_spec=pltpu.PrefetchScalarGridSpec(
            num_scalar_prefetch=3,
            grid=(16,),
            in_specs=[spec(0), spec(1)],
            out_specs=(
                pl.BlockSpec((1, 256, 1024), lambda s, t, c, n: (s, 0, 0)),
                pl.BlockSpec((1024, 256), lambda s, t, c, n: (0, (s % RING) * 2 + s // RING)),
            ),
        ),
        compiler_params=pltpu.CompilerParams(vmem_limit_bytes=24 << 20),
    )(table, cols, count, blocks, blocks)


VM = pl.BlockSpec(memory_space=pltpu.VMEM)


def spread_kernel(lo, n, final, turned, *refs):
    parts, held, outs = refs[:n], refs[-1], refs[n:-1]
    at = 0
    for part in parts:
        held[at : at + part.shape[0], :] = part[...]
        at += part.shape[0]
    if not final:
        outs[0][...] = jnp.dot(turned[:, lo : lo + at], held[...], preferred_element_type=F32)
        return
    for d in range(ROWS):
        rows = slice(d * 128, d * 128 + 128)
        value = jnp.dot(turned[rows, lo : lo + at], held[...], preferred_element_type=F32)
        outs[1 + d][...] = (value + outs[0][rows, :]).astype(outs[1 + d].dtype)


def spread(turned, lo, parts, before=None):
    width = sum(p.shape[0] for p in parts)
    final = before is not None
    shapes = [jax.ShapeDtypeStruct((128, 768), F32 if d == 0 else BF16) for d in range(ROWS)]
    if not final:
        shapes = [jax.ShapeDtypeStruct((1024, 768), F32)]
    args = [turned, *parts] + ([before] if final else [])
    return pl.pallas_call(
        functools.partial(spread_kernel, lo, len(parts), final),
        out_shape=shapes,
        in_specs=[VM] * len(args),
        out_specs=[VM] * len(shapes),
        scratch_shapes=[pltpu.VMEM((width, 768), BF16)],
        compiler_params=pltpu.CompilerParams(vmem_limit_bytes=40 << 20),
    )(*args)


def weight_kernel(table, own, summed, *refs):
    out = refs[-1]
    total = jnp.zeros(out.shape, F32)
    k = 0
    for grads in refs[:-1]:
        count = grads.shape[0] // 128
        left = jnp.concatenate(
            [
                jnp.concatenate([own[table[k + i]], summed[table[k + i]]], axis=0)
                for i in range(count)
            ],
            axis=1,
        )
        k += count
        total += jnp.dot(left, grads[...], preferred_element_type=F32)
    out[...] = total


def weight_slices(table, own, summed, grads):
    return pl.pallas_call(
        weight_kernel,
        out_shape=jax.ShapeDtypeStruct((96, 768), F32),
        in_specs=[pl.BlockSpec(memory_space=pltpu.SMEM)] + [VM] * (2 + len(grads)),
        out_specs=VM,
        compiler_params=pltpu.CompilerParams(vmem_limit_bytes=24 << 20),
    )(table, own, summed, *grads)


def silu_slope(hidden):
    sigmoid_value = jax.nn.sigmoid(hidden)
    return sigmoid_value * (1.0 + hidden * (1.0 - sigmoid_value))


def dot(a, b):
    return jnp.dot(a, b, preferred_element_type=F32)


def per_device(features, cotangent, w_self, w_neigh, degree, block_cols, block_count, blocks):
    row, col = lax.axis_index("row"), lax.axis_index("col")
    core, ring, far = col % 2, (col // 2) % RING, col // 16
    offsets = jnp.array(OFFSETS, jnp.int32)
    ring_at = (ring + offsets) % RING
    core_at = jnp.arange(2, dtype=jnp.int32) ^ core
    far_at = jnp.arange(2, dtype=jnp.int32) ^ far
    table = (
        far_at[None, None, :] * 16 + ring_at[None, :, None] * 2 + core_at[:, None, None]
    ).reshape(-1)
    group_at = (far_at[None, :] * RING + ring_at[:, None]).reshape(-1)
    dense, turned = place(table, (block_cols[0, 0] ^ row).reshape(-1), block_count[0, 0], blocks[0, 0])
    dense = dense.reshape(2, RING, 256, 1024)

    degree_f = degree.astype(F32)[:, None]
    pieces = [features] + [to_row(features, d) for d in range(1, ROWS)]
    own_t = (features.astype(F32) * degree_f).astype(BF16).T
    own_slices = lax.all_to_all(
        own_t.reshape(16, 48, 128), "col", 0, 0, axis_index_groups=column_groups(), tiled=True
    )
    self_part = dot(features, w_self)
    pieces, own_slices, dense, turned, self_part = lax.optimization_barrier(
        (pieces, own_slices, dense, turned, self_part)
    )
    sources = jnp.concatenate(pieces, axis=0)

    mine = {}

    def pair_sums(lo, hi, sources):
        sent = dot(dense[1, lo:hi].reshape(-1, 1024), sources).astype(BF16)
        got = to_partner(sent).astype(F32)
        kept = dot(dense[0, lo:hi].reshape(-1, 1024), sources) + got
        for k in range(lo, hi):
            mine[OFFSETS[k]] = kept[(k - lo) * 256 : (k - lo + 1) * 256]

    pair_sums(0, 1, sources)
    first = (mine[4][:128].astype(BF16), mine[4][128:].astype(BF16))
    first, sources = lax.optimization_barrier((first, sources))
    for lo, hi in ((1, 3), (3, 5), (5, 8)):
        pair_sums(lo, hi, sources)
    up, down = along(first[0], 1), along(first[1], -1)
    up = jnp.concatenate([mine[3][:128] + up.astype(F32), mine[3][128:]], axis=0)
    down = jnp.concatenate([mine[5][:128], mine[5][128:] + down.astype(F32)], axis=0)
    for reach in (2, 1, 0):
        up, down = along(up.astype(BF16), 1), along(down.astype(BF16), -1)
        if reach:
            up = mine[reach] + up.astype(F32)
            down = mine[RING - reach] + down.astype(F32)
    ends = mine[0] + up.astype(F32) + down.astype(F32)
    summed = ends[:128] + to_far(ends[128:].astype(BF16)).astype(F32)

    aggregate = (summed / degree_f).astype(BF16)
    hidden = self_part + dot(aggregate, w_neigh)
    output = jax.nn.silu(hidden).astype(BF16)
    slope = cotangent.astype(F32) * silu_slope(hidden)
    hidden_grad = slope.astype(BF16)
    shared = (slope / degree_f).astype(BF16)

    shared = jnp.concatenate([shared, to_far(shared)], axis=0)
    held = {0: (shared,)}
    up = down = shared
    for reach in (1, 2, 3):
        up, down = along(up, 1), along(down, -1)
        held[RING - reach], held[reach] = (up,), (down,)
    held[4] = (along(up[:128], 1), along(down[128:], -1))
    there = {o: tuple(to_partner(p) for p in held[o]) for o in held}
    summed_slices = lax.all_to_all(
        summed.astype(BF16).T.reshape(16, 48, 128), "col", 0, 0, axis_index_groups=column_groups(), tiled=True
    )
    (before,) = spread(turned, 6 * 256, [p for o in OFFSETS[3:] for p in held[o] + there[o]])
    chunks = spread(turned, 0, [p for o in OFFSETS[:3] for p in held[o] + there[o]], before)
    back = chunks[0]
    for d in range(1, ROWS):
        back = back + to_row(chunks[d], d).astype(F32)
    against = (((1,), (1,)), ((), ()))
    grad_features = (
        lax.dot_general(hidden_grad, w_self, against, preferred_element_type=F32)
        + lax.dot_general(back.astype(BF16), w_neigh, against, preferred_element_type=F32)
    ).astype(BF16)

    slices = weight_slices(
        group_at, own_slices, summed_slices, [p for o in OFFSETS for p in held[o]]
    )
    slices = slices.reshape(2, 48, 768)
    kept = lax.dynamic_index_in_dim(slices, core, 0, keepdims=False)
    sent = lax.dynamic_index_in_dim(slices, 1 - core, 0, keepdims=False)
    pair = (kept + to_partner(sent)).astype(BF16)
    rows_all = lax.all_to_all(
        jnp.broadcast_to(pair[None], (ROWS, 48, 768)), "row", 0, 0, tiled=True
    )
    grad_scale = float(128 * ROWS * COLS) ** (-0.5)
    total = (jnp.sum(rows_all.astype(F32), axis=0) * grad_scale).astype(BF16)
    full = lax.all_to_all(
        jnp.broadcast_to(total[None], (16, 48, 768)), "col", 0, 0, axis_index_groups=column_groups(), tiled=True
    ).reshape(768, 768)
    other = to_partner(full)
    grad_w_self = jnp.where(core == 0, full, other).astype(F32)
    grad_w_neigh = jnp.where(core == 0, other, full).astype(F32)
    return (output, grad_features, grad_w_self, grad_w_neigh)


def solution(mesh):
    placed = (
        P(("row", "col"), None),
        P(("row", "col"), None),
        P(),
        P(),
        P(("row", "col")),
        P("row", "col", None, None),
        P("row", "col", None),
        P("row", "col", None, None, None, None),
    )
    return jax.shard_map(
        per_device,
        mesh=mesh,
        in_specs=placed,
        out_specs=(P(("row", "col"), None), P(("row", "col"), None), P(), P()),
        check_vma=False,
    )
```

```python
import functools

import jax
import jax.numpy as jnp
from jax import lax
from jax.experimental import pallas as pl
from jax.experimental.pallas import tpu as pltpu
from jax.sharding import PartitionSpec as P

ROWS, COLS, RING = 8, 32, 8
OFFSETS = (4, 3, 5, 2, 6, 1, 7, 0)
F32, BF16 = jnp.float32, jnp.bfloat16


def to_partner(value):
    return lax.ppermute(value, "col", [(j, j ^ 1) for j in range(COLS)])


def to_far(value):
    return lax.ppermute(value, "col", [(j, j ^ 16) for j in range(COLS)])


def along(value, step):
    pairs = [(j, (j & 17) | (((j // 2 + step) % RING) * 2)) for j in range(COLS)]
    return lax.ppermute(value, "col", pairs)


def to_row(value, flip):
    return lax.ppermute(value, "row", [(i, i ^ flip) for i in range(ROWS)])


def column_groups():
    return [[c for c in range(COLS) if c % 2 == k] for k in range(2)]


def turn_kernel(table, cols, count, first, second, turned):
    step = pl.program_id(0)
    turned[...] = jnp.zeros_like(turned)
    for part, blocks in enumerate((first, second)):
        row = table[(step % 2) * 16 + (step // 2) * 2 + part]
        for slot in range(4):
            @pl.when(slot < count[row])
            def _():
                at = pl.multiple_of(cols[row * 4 + slot] * 128, 128)
                turned[pl.ds(at, 128), part * 128 : part * 128 + 128] = blocks[0, slot].T


def turn(lists, blocks):
    def spec(part):
        return pl.BlockSpec(
            (1, 4, 128, 128), lambda s, t, c, n: (t[(s % 2) * 16 + (s // 2) * 2 + part], 0, 0, 0)
        )

    return pl.pallas_call(
        turn_kernel,
        out_shape=jax.ShapeDtypeStruct((1024, 4096), BF16),
        grid_spec=pltpu.PrefetchScalarGridSpec(
            num_scalar_prefetch=3,
            grid=(16,),
            in_specs=[spec(0), spec(1)],
            out_specs=pl.BlockSpec((1024, 256), lambda s, t, c, n: (0, s)),
        ),
        compiler_params=pltpu.CompilerParams(vmem_limit_bytes=24 << 20),
    )(*lists, blocks, blocks)


def sums_kernel(start, crossed, table, cols, count, first, second, *refs):
    pieces, rest = refs[:ROWS], refs[ROWS:]
    out, sources, dense = rest[-3:]
    step = pl.program_id(0)

    @pl.when(step == 0)
    def _():
        for d in range(ROWS):
            sources[d * 128 : d * 128 + 128, :] = pieces[d][...]

    dense[...] = jnp.zeros_like(dense)
    for part, blocks in enumerate((first, second)):
        row = table[start + step * 2 + part]
        for slot in range(4):
            @pl.when(slot < count[row])
            def _():
                at = pl.multiple_of(cols[row * 4 + slot] * 128, 128)
                dense[part * 128 : part * 128 + 128, pl.ds(at, 128)] = blocks[0, slot]
    value = jnp.dot(dense[...], sources[...], preferred_element_type=F32)
    if crossed:
        value = value + rest[0][...].astype(F32)
    out[...] = value.astype(out.dtype)


def sums(lists, blocks, pieces, side, lo, hi, crossed=None):
    start = side * 16 + lo * 2

    def spec(part):
        return pl.BlockSpec((1, 4, 128, 128), lambda s, t, c, n: (t[start + s * 2 + part], 0, 0, 0))

    line = pl.BlockSpec((256, 768), lambda s, t, c, n: (s, 0))
    whole = pl.BlockSpec((128, 768), lambda s, t, c, n: (0, 0))
    added = [] if crossed is None else [crossed]
    return pl.pallas_call(
        functools.partial(sums_kernel, start, crossed is not None),
        out_shape=jax.ShapeDtypeStruct(((hi - lo) * 256, 768), BF16 if crossed is None else F32),
        grid_spec=pltpu.PrefetchScalarGridSpec(
            num_scalar_prefetch=3,
            grid=(hi - lo,),
            in_specs=[spec(0), spec(1)] + [whole] * ROWS + [line] * len(added),
            out_specs=line,
            scratch_shapes=[pltpu.VMEM((1024, 768), BF16), pltpu.VMEM((256, 1024), BF16)],
        ),
        compiler_params=pltpu.CompilerParams(vmem_limit_bytes=24 << 20),
    )(*lists, blocks, blocks, *pieces, *added)


VM = pl.BlockSpec(memory_space=pltpu.VMEM)


def spread_kernel(lo, n, added, final, turned, *refs):
    parts, held, outs = refs[:n], refs[-1], refs[n:-1]
    at = 0
    for part in parts:
        held[at : at + part.shape[0], :] = part[...]
        at += part.shape[0]
    if not final:
        value = jnp.dot(turned[:, lo : lo + at], held[...], preferred_element_type=F32)
        outs[-1][...] = value + outs[0][...] if added else value
        return
    for d in range(ROWS):
        rows = slice(d * 128, d * 128 + 128)
        value = jnp.dot(turned[rows, lo : lo + at], held[...], preferred_element_type=F32)
        outs[1 + d][...] = (value + outs[0][rows, :]).astype(outs[1 + d].dtype)


def spread(turned, lo, parts, before=None, final=False):
    width = sum(p.shape[0] for p in parts)
    added = before is not None
    shapes = [jax.ShapeDtypeStruct((128, 768), F32 if d == 0 else BF16) for d in range(ROWS)]
    if not final:
        shapes = [jax.ShapeDtypeStruct((1024, 768), F32)]
    args = [turned, *parts] + ([before] if added else [])
    return pl.pallas_call(
        functools.partial(spread_kernel, lo, len(parts), added, final),
        out_shape=shapes,
        in_specs=[VM] * len(args),
        out_specs=[VM] * len(shapes),
        scratch_shapes=[pltpu.VMEM((width, 768), BF16)],
        compiler_params=pltpu.CompilerParams(vmem_limit_bytes=40 << 20),
    )(*args)


def silu_slope(hidden):
    sigmoid_value = jax.nn.sigmoid(hidden)
    return sigmoid_value * (1.0 + hidden * (1.0 - sigmoid_value))


def dot(a, b):
    return jnp.dot(a, b, preferred_element_type=F32)


def per_device(features, cotangent, w_self, w_neigh, degree, block_cols, block_count, blocks):
    row, col = lax.axis_index("row"), lax.axis_index("col")
    core, ring, far = col % 2, (col // 2) % RING, col // 16
    offsets = jnp.array(OFFSETS, jnp.int32)
    ring_at = (ring + offsets) % RING
    core_at = jnp.arange(2, dtype=jnp.int32) ^ core
    far_at = jnp.arange(2, dtype=jnp.int32) ^ far
    table = (
        far_at[None, None, :] * 16 + ring_at[None, :, None] * 2 + core_at[:, None, None]
    ).reshape(-1)
    lists = (table, (block_cols[0, 0] ^ row).reshape(-1), block_count[0, 0])
    tile_blocks = blocks[0, 0]
    degree_f = degree.astype(F32)[:, None]
    pieces = [features] + [None] * 7
    for d in (1, 2, 6, 4):
        pieces[d] = to_row(features, d)
    for d in (2, 6, 4):
        pieces[d ^ 1] = to_row(pieces[1], d)
    lists, _ = lax.optimization_barrier((lists, pieces[1]))
    turned = turn(lists, tile_blocks)
    self_part = dot(features, w_self)
    pieces, turned, self_part = lax.optimization_barrier((pieces, turned, self_part))

    sent = sums(lists, tile_blocks, pieces, 1, 0, 1)
    got = to_partner(sent)
    sent, pieces = lax.optimization_barrier((sent, pieces))
    sent2 = sums(lists, tile_blocks, pieces, 1, 1, 3)
    got2 = to_partner(sent2)
    sent2, pieces = lax.optimization_barrier((sent2, pieces))
    far4 = sums(lists, tile_blocks, pieces, 0, 0, 1, got)
    up, down, pieces = lax.optimization_barrier(
        (far4[:128].astype(BF16), far4[128:].astype(BF16), pieces)
    )
    up, down = along(up, 1), along(down, -1)
    near3 = sums(lists, tile_blocks, pieces, 0, 1, 3, got2)
    near3, pieces = lax.optimization_barrier((near3, pieces))
    sent3 = sums(lists, tile_blocks, pieces, 1, 3, 5)
    got3 = to_partner(sent3)
    up = jnp.concatenate([near3[:128] + up.astype(F32), near3[128:256]], axis=0).astype(BF16)
    down = jnp.concatenate([near3[256:384], near3[384:] + down.astype(F32)], axis=0).astype(BF16)
    up, down, sent3, pieces = lax.optimization_barrier((up, down, sent3, pieces))
    up, down = along(up, 1), along(down, -1)
    sent4 = sums(lists, tile_blocks, pieces, 1, 5, 8)
    got4 = to_partner(sent4)
    sent4, pieces = lax.optimization_barrier((sent4, pieces))
    near2 = sums(lists, tile_blocks, pieces, 0, 3, 5, got3)
    up = (near2[:256] + up.astype(F32)).astype(BF16)
    down = (near2[256:] + down.astype(F32)).astype(BF16)
    up, down, pieces = lax.optimization_barrier((up, down, pieces))
    up, down = along(up, 1), along(down, -1)
    near = sums(lists, tile_blocks, pieces, 0, 5, 8, got4)
    up = (near[:256] + up.astype(F32)).astype(BF16)
    down = (near[256:512] + down.astype(F32)).astype(BF16)
    up, down, near = lax.optimization_barrier((up, down, near))
    up, down = along(up, 1), along(down, -1)
    ends = near[512:] + up.astype(F32) + down.astype(F32)
    summed = ends[:128] + to_far(ends[128:].astype(BF16)).astype(F32)

    aggregate = (summed / degree_f).astype(BF16)
    hidden = self_part + dot(aggregate, w_neigh)
    output = jax.nn.silu(hidden).astype(BF16)
    slope = cotangent.astype(F32) * silu_slope(hidden)
    hidden_grad = slope.astype(BF16)
    shared = (slope / degree_f).astype(BF16)

    across = (((0,), (0,)), ((), ()))
    kept = jnp.where(core == 0, features, aggregate)
    given = jnp.where(core == 0, aggregate, features)
    given = lax.dot_general(given, hidden_grad, across, preferred_element_type=F32).astype(BF16)
    far_shared = to_far(shared)
    pair = lax.dot_general(kept, hidden_grad, across, preferred_element_type=F32)
    shared, given, pair = lax.optimization_barrier(
        (jnp.concatenate([shared, far_shared], axis=0), given, pair)
    )

    held, there = {0: (shared,)}, {}
    given = to_partner(given)
    up, down = along(shared, 1), along(shared, -1)
    up, down, given = lax.optimization_barrier((up, down, given))
    held[7], held[1] = (up,), (down,)
    pair = (pair + given.astype(F32)).astype(BF16)
    part = lax.all_to_all(pair.reshape(ROWS, 96, 768), "row", 0, 0, tiled=True)
    up, down = along(up, 1), along(down, -1)
    up, down, part = lax.optimization_barrier((up, down, part))
    held[6], held[2] = (up,), (down,)
    for o in (0, 7, 1, 6, 2):
        there[o] = tuple(to_partner(p) for p in held[o])
    (before,) = spread(turned, 6 * 256, [p for o in OFFSETS[3:] for p in held[o] + there[o]])
    up, down = along(up, 1), along(down, -1)
    up, down, part, before = lax.optimization_barrier((up, down, part, before))
    held[5], held[3] = (up,), (down,)
    part = jnp.sum(part.astype(F32), axis=0).astype(BF16)
    part = lax.all_to_all(
        part.reshape(16, 6, 768), "col", 0, 0, axis_index_groups=column_groups(), tiled=True
    )
    held[4] = (along(up[:128], 1), along(down[128:], -1))
    for o in (5, 3):
        there[o] = tuple(to_partner(p) for p in held[o])
    (before,) = spread(turned, 2 * 256, [p for o in OFFSETS[1:3] for p in held[o] + there[o]], before)
    held[4], before, part = lax.optimization_barrier((held[4], before, part))
    grad_scale = float(128 * ROWS * COLS) ** (-0.5)
    part = (jnp.sum(part.astype(F32), axis=0) * grad_scale).astype(BF16)
    part = lax.all_to_all(
        jnp.broadcast_to(part[None], (16, 6, 768)), "col", 0, 0, axis_index_groups=column_groups(), tiled=True
    ).reshape(96, 768)
    there[4] = tuple(to_partner(p) for p in held[4])
    chunks = spread(turned, 0, held[4] + there[4], before, True)
    early = [to_row(chunks[d], d) for d in (1, 2, 6)]
    early, part = lax.optimization_barrier((early, part))
    full = lax.all_to_all(jnp.broadcast_to(part[None], (ROWS, 96, 768)), "row", 0, 0, tiled=True)
    arrived = early + [to_row(chunks[d], d) for d in (4, 3, 7, 5)]
    full = full.reshape(768, 768)
    other = to_partner(full)
    grad_w_self = jnp.where(core == 0, full, other).astype(F32)
    grad_w_neigh = jnp.where(core == 0, other, full).astype(F32)
    arrived[3:], grad_w_self, grad_w_neigh = lax.optimization_barrier(
        (arrived[3:], grad_w_self, grad_w_neigh)
    )
    back = chunks[0]
    for value in arrived:
        back = back + value.astype(F32)
    against = (((1,), (1,)), ((), ()))
    grad_features = (
        lax.dot_general(hidden_grad, w_self, against, preferred_element_type=F32)
        + lax.dot_general(back.astype(BF16), w_neigh, against, preferred_element_type=F32)
    ).astype(BF16)
    return (output, grad_features, grad_w_self, grad_w_neigh)


def solution(mesh):
    placed = (
        P(("row", "col"), None),
        P(("row", "col"), None),
        P(),
        P(),
        P(("row", "col")),
        P("row", "col", None, None),
        P("row", "col", None),
        P("row", "col", None, None, None, None),
    )
    return jax.shard_map(
        per_device,
        mesh=mesh,
        in_specs=placed,
        out_specs=(P(("row", "col"), None), P(("row", "col"), None), P(), P()),
        check_vma=False,
    )
```

```python
import functools

import jax
import jax.numpy as jnp
from jax import lax
from jax.experimental import pallas as pl
from jax.experimental.pallas import tpu as pltpu
from jax.sharding import PartitionSpec as P

ROWS, COLS, RING = 8, 32, 8
OFFSETS = (4, 3, 5, 2, 6, 1, 7, 0)
F32, BF16 = jnp.float32, jnp.bfloat16


def to_partner(value):
    return lax.ppermute(value, "col", [(j, j ^ 1) for j in range(COLS)])


def to_far(value):
    return lax.ppermute(value, "col", [(j, j ^ 16) for j in range(COLS)])


def along(value, step):
    pairs = [(j, (j & 17) | (((j // 2 + step) % RING) * 2)) for j in range(COLS)]
    return lax.ppermute(value, "col", pairs)


def to_row(value, flip):
    return lax.ppermute(value, "row", [(i, i ^ flip) for i in range(ROWS)])


def column_groups():
    return [[c for c in range(COLS) if c % 2 == k] for k in range(2)]


def turn_kernel(lo, table, cols, count, first, second, turned):
    step = pl.program_id(0) + lo * 2
    turned[...] = jnp.zeros_like(turned)
    for part, blocks in enumerate((first, second)):
        row = table[(step % 2) * 16 + (step // 2) * 2 + part]
        for slot in range(4):
            @pl.when(slot < count[row])
            def _():
                at = pl.multiple_of(cols[row * 4 + slot] * 128, 128)
                turned[pl.ds(at, 128), part * 128 : part * 128 + 128] = blocks[0, slot].T


def turn(lists, blocks, lo, hi):
    def spec(part):
        return pl.BlockSpec(
            (1, 4, 128, 128),
            lambda s, t, c, n: (t[(s % 2) * 16 + (s // 2 + lo) * 2 + part], 0, 0, 0),
        )

    return pl.pallas_call(
        functools.partial(turn_kernel, lo),
        out_shape=jax.ShapeDtypeStruct((1024, (hi - lo) * 512), BF16),
        grid_spec=pltpu.PrefetchScalarGridSpec(
            num_scalar_prefetch=3,
            grid=((hi - lo) * 2,),
            in_specs=[spec(0), spec(1)],
            out_specs=pl.BlockSpec((1024, 256), lambda s, t, c, n: (0, s)),
        ),
        compiler_params=pltpu.CompilerParams(vmem_limit_bytes=12 << 20),
    )(*lists, blocks, blocks)


def sums_kernel(start, crossed, table, cols, count, first, second, *refs):
    pieces, rest = refs[:ROWS], refs[ROWS:]
    out, sources, dense = rest[-3:]
    step = pl.program_id(0)

    @pl.when(step == 0)
    def _():
        for d in range(ROWS):
            sources[d * 128 : d * 128 + 128, :] = pieces[d][...]

    dense[...] = jnp.zeros_like(dense)
    for part, blocks in enumerate((first, second)):
        row = table[start + step * 2 + part]
        for slot in range(4):
            @pl.when(slot < count[row])
            def _():
                at = pl.multiple_of(cols[row * 4 + slot] * 128, 128)
                dense[part * 128 : part * 128 + 128, pl.ds(at, 128)] = blocks[0, slot]
    value = jnp.dot(dense[...], sources[...], preferred_element_type=F32)
    if crossed:
        value = value + rest[0][...].astype(F32)
    out[...] = value.astype(out.dtype)


def sums(lists, blocks, pieces, side, lo, hi, crossed=None):
    start = side * 16 + lo * 2

    def spec(part):
        return pl.BlockSpec((1, 4, 128, 128), lambda s, t, c, n: (t[start + s * 2 + part], 0, 0, 0))

    line = pl.BlockSpec((256, 768), lambda s, t, c, n: (s, 0))
    whole = pl.BlockSpec((128, 768), lambda s, t, c, n: (0, 0))
    added = [] if crossed is None else [crossed]
    return pl.pallas_call(
        functools.partial(sums_kernel, start, crossed is not None),
        out_shape=jax.ShapeDtypeStruct(((hi - lo) * 256, 768), BF16 if crossed is None else F32),
        grid_spec=pltpu.PrefetchScalarGridSpec(
            num_scalar_prefetch=3,
            grid=(hi - lo,),
            in_specs=[spec(0), spec(1)] + [whole] * ROWS + [line] * len(added),
            out_specs=line,
            scratch_shapes=[pltpu.VMEM((1024, 768), BF16), pltpu.VMEM((256, 1024), BF16)],
        ),
        compiler_params=pltpu.CompilerParams(vmem_limit_bytes=12 << 20),
    )(*lists, blocks, blocks, *pieces, *added)


VM = pl.BlockSpec(memory_space=pltpu.VMEM)


def stack(parts, held):
    at = 0
    for part in parts:
        held[at : at + part.shape[0], :] = part[...]
        at += part.shape[0]
    return at


def spread_kernel(lo, n, added, turned, *refs):
    parts, out, held = refs[:n], refs[-2], refs[-1]
    width = stack(parts, held)
    value = jnp.dot(turned[:, lo : lo + width], held[...], preferred_element_type=F32)
    out[...] = value + refs[n][...] if added else value


def spread(turned, lo, parts, before=None):
    args = [turned, *parts] + ([] if before is None else [before])
    return pl.pallas_call(
        functools.partial(spread_kernel, lo, len(parts), before is not None),
        out_shape=jax.ShapeDtypeStruct((1024, 768), F32),
        in_specs=[VM] * len(args),
        out_specs=VM,
        scratch_shapes=[pltpu.VMEM((sum(p.shape[0] for p in parts), 768), BF16)],
        compiler_params=pltpu.CompilerParams(vmem_limit_bytes=20 << 20),
    )(*args)


def last_kernel(n, place, turned, before, extra, *refs):
    parts, out, held = refs[:n], refs[-2], refs[-1]
    width = stack(parts, held)
    for d in range(ROWS):
        rows = slice(d * 128, d * 128 + 128)
        value = jnp.dot(turned[rows, :width], held[...], preferred_element_type=F32)
        out[place[d], :128, :] = (value + before[rows, :]).astype(BF16)
        out[d, 128:, :] = extra[...]


def last_spread(place, turned, parts, before, extra):
    return pl.pallas_call(
        functools.partial(last_kernel, len(parts)),
        out_shape=jax.ShapeDtypeStruct((ROWS, 128 + extra.shape[0], 768), BF16),
        in_specs=[pl.BlockSpec(memory_space=pltpu.SMEM)] + [VM] * (3 + len(parts)),
        out_specs=VM,
        scratch_shapes=[pltpu.VMEM((sum(p.shape[0] for p in parts), 768), BF16)],
        compiler_params=pltpu.CompilerParams(vmem_limit_bytes=20 << 20),
    )(place, turned, before, extra, *parts)


def silu_slope(hidden):
    sigmoid_value = jax.nn.sigmoid(hidden)
    return sigmoid_value * (1.0 + hidden * (1.0 - sigmoid_value))


def dot(a, b):
    return jnp.dot(a, b, preferred_element_type=F32)


def per_device(features, cotangent, w_self, w_neigh, degree, block_cols, block_count, blocks):
    row, col = lax.axis_index("row"), lax.axis_index("col")
    core, ring, far = col % 2, (col // 2) % RING, col // 16
    offsets = jnp.array(OFFSETS, jnp.int32)
    ring_at = (ring + offsets) % RING
    core_at = jnp.arange(2, dtype=jnp.int32) ^ core
    far_at = jnp.arange(2, dtype=jnp.int32) ^ far
    table = (
        far_at[None, None, :] * 16 + ring_at[None, :, None] * 2 + core_at[:, None, None]
    ).reshape(-1)
    lists = (table, (block_cols[0, 0] ^ row).reshape(-1), block_count[0, 0])
    tile_blocks = blocks[0, 0]
    degree_f = degree.astype(F32)[:, None]
    pieces = [features] + [None] * 7
    for d in (1, 2, 6, 4):
        pieces[d] = to_row(features, d)
    for d in (2, 6, 4):
        pieces[d ^ 1] = to_row(pieces[1], d)
    self_part = dot(features, w_self)
    pieces, self_part = lax.optimization_barrier((pieces, self_part))

    sent = sums(lists, tile_blocks, pieces, 1, 0, 1)
    got = to_partner(sent)
    sent, pieces = lax.optimization_barrier((sent, pieces))
    sent2 = sums(lists, tile_blocks, pieces, 1, 1, 3)
    got2 = to_partner(sent2)
    sent2, pieces = lax.optimization_barrier((sent2, pieces))
    far4 = sums(lists, tile_blocks, pieces, 0, 0, 1, got)
    up, down, pieces = lax.optimization_barrier(
        (far4[:128].astype(BF16), far4[128:].astype(BF16), pieces)
    )
    up, down = along(up, 1), along(down, -1)
    near3 = sums(lists, tile_blocks, pieces, 0, 1, 3, got2)
    near3, pieces = lax.optimization_barrier((near3, pieces))
    sent3 = sums(lists, tile_blocks, pieces, 1, 3, 5)
    got3 = to_partner(sent3)
    up = jnp.concatenate([near3[:128] + up.astype(F32), near3[128:256]], axis=0).astype(BF16)
    down = jnp.concatenate([near3[256:384], near3[384:] + down.astype(F32)], axis=0).astype(BF16)
    up, down, sent3, pieces = lax.optimization_barrier((up, down, sent3, pieces))
    up, down = along(up, 1), along(down, -1)
    sent4 = sums(lists, tile_blocks, pieces, 1, 5, 8)
    got4 = to_partner(sent4)
    sent4, pieces = lax.optimization_barrier((sent4, pieces))
    near2 = sums(lists, tile_blocks, pieces, 0, 3, 5, got3)
    up = (near2[:256] + up.astype(F32)).astype(BF16)
    down = (near2[256:] + down.astype(F32)).astype(BF16)
    up, down, pieces, lists = lax.optimization_barrier((up, down, pieces, lists))
    up, down = along(up, 1), along(down, -1)
    turned_late = turn(lists, tile_blocks, 0, 3)
    near = sums(lists, tile_blocks, pieces, 0, 5, 8, got4)
    up = (near[:256] + up.astype(F32)).astype(BF16)
    down = (near[256:512] + down.astype(F32)).astype(BF16)
    up, down, near, lists, turned_late = lax.optimization_barrier((up, down, near, lists, turned_late))
    up, down = along(up, 1), along(down, -1)
    turned = turn(lists, tile_blocks, 3, 8)
    up, down, turned = lax.optimization_barrier((up, down, turned))
    ends = near[512:] + up.astype(F32) + down.astype(F32)
    summed = ends[:128] + to_far(ends[128:].astype(BF16)).astype(F32)

    aggregate = (summed / degree_f).astype(BF16)
    hidden = self_part + dot(aggregate, w_neigh)
    output = jax.nn.silu(hidden).astype(BF16)
    slope = cotangent.astype(F32) * silu_slope(hidden)
    hidden_grad = slope.astype(BF16)
    shared = (slope / degree_f).astype(BF16)

    across = (((0,), (0,)), ((), ()))
    kept = jnp.where(core == 0, features, aggregate)
    given = jnp.where(core == 0, aggregate, features)
    given = lax.dot_general(given, hidden_grad, across, preferred_element_type=F32).astype(BF16)
    far_shared = to_far(shared)
    pair = lax.dot_general(kept, hidden_grad, across, preferred_element_type=F32)
    shared, given, pair = lax.optimization_barrier(
        (jnp.concatenate([shared, far_shared], axis=0), given, pair)
    )

    held, there = {0: (shared,)}, {}
    given = to_partner(given)
    up, down = along(shared, 1), along(shared, -1)
    up, down, given = lax.optimization_barrier((up, down, given))
    held[7], held[1] = (up,), (down,)
    pair = (pair + given.astype(F32)).astype(BF16)
    part = lax.all_to_all(pair.reshape(ROWS, 96, 768), "row", 0, 0, tiled=True)
    up, down = along(up, 1), along(down, -1)
    held[6], held[2] = (up,), (down,)
    for o in (0, 7, 1, 6, 2):
        there[o] = tuple(to_partner(p) for p in held[o])
    before = spread(turned, 0, [p for o in OFFSETS[3:] for p in held[o] + there[o]])
    up, down = along(up, 1), along(down, -1)
    up, down, part, before = lax.optimization_barrier((up, down, part, before))
    held[5], held[3] = (up,), (down,)
    part = jnp.sum(part.astype(F32), axis=0).astype(BF16)
    part = lax.all_to_all(
        part.reshape(16, 6, 768), "col", 0, 0, axis_index_groups=column_groups(), tiled=True
    )
    held[4] = (along(up[:128], 1), along(down[128:], -1))
    for o in (5, 3):
        there[o] = tuple(to_partner(p) for p in held[o])
    before = spread(turned_late, 2 * 256, [p for o in OFFSETS[1:3] for p in held[o] + there[o]], before)
    held[4], before, part = lax.optimization_barrier((held[4], before, part))
    there[4] = tuple(to_partner(p) for p in held[4])
    grad_scale = float(128 * ROWS * COLS) ** (-0.5)
    part = (jnp.sum(part.astype(F32), axis=0) * grad_scale).astype(BF16)
    part = lax.all_to_all(
        jnp.broadcast_to(part[None], (16, 6, 768)), "col", 0, 0, axis_index_groups=column_groups(), tiled=True
    ).reshape(96, 768)
    place = jnp.arange(ROWS, dtype=jnp.int32) ^ row
    mixed = last_spread(place, turned_late, held[4] + there[4], before, part)
    mixed = lax.all_to_all(mixed, "row", 0, 0, tiled=True)
    full = mixed[:, 128:].reshape(768, 768)
    other = to_partner(full)
    grad_w_self = jnp.where(core == 0, full, other).astype(F32)
    grad_w_neigh = jnp.where(core == 0, other, full).astype(F32)
    back = jnp.sum(mixed[:, :128].astype(F32), axis=0)
    against = (((1,), (1,)), ((), ()))
    grad_features = (
        lax.dot_general(hidden_grad, w_self, against, preferred_element_type=F32)
        + lax.dot_general(back.astype(BF16), w_neigh, against, preferred_element_type=F32)
    ).astype(BF16)
    return (output, grad_features, grad_w_self, grad_w_neigh)


def solution(mesh):
    placed = (
        P(("row", "col"), None),
        P(("row", "col"), None),
        P(),
        P(),
        P(("row", "col")),
        P("row", "col", None, None),
        P("row", "col", None),
        P("row", "col", None, None, None, None),
    )
    return jax.shard_map(
        per_device,
        mesh=mesh,
        in_specs=placed,
        out_specs=(P(("row", "col"), None), P(("row", "col"), None), P(), P()),
        check_vma=False,
    )
```

```python
import functools

import jax
import jax.numpy as jnp
from jax import lax
from jax.experimental import pallas as pl
from jax.experimental.pallas import tpu as pltpu
from jax.sharding import PartitionSpec as P

ROWS, COLS, RING = 8, 32, 8
OFFSETS = (4, 3, 5, 2, 6, 1, 7, 0)
F32, BF16 = jnp.float32, jnp.bfloat16


def to_partner(value):
    return lax.ppermute(value, "col", [(j, j ^ 1) for j in range(COLS)])


def to_far(value):
    return lax.ppermute(value, "col", [(j, j ^ 16) for j in range(COLS)])


def along(value, step):
    pairs = [(j, (j & 17) | (((j // 2 + step) % RING) * 2)) for j in range(COLS)]
    return lax.ppermute(value, "col", pairs)


def to_row(value, flip):
    return lax.ppermute(value, "row", [(i, i ^ flip) for i in range(ROWS)])


def column_groups():
    return [[c for c in range(COLS) if c % 2 == k] for k in range(2)]


def turn_kernel(lo, table, cols, count, first, second, turned):
    step = pl.program_id(0) + lo * 2
    turned[...] = jnp.zeros_like(turned)
    for part, blocks in enumerate((first, second)):
        row = table[(step % 2) * 16 + (step // 2) * 2 + part]
        for slot in range(4):
            @pl.when(slot < count[row])
            def _():
                at = pl.multiple_of(cols[row * 4 + slot] * 128, 128)
                turned[pl.ds(at, 128), part * 128 : part * 128 + 128] = blocks[0, slot].T


def turn(lists, blocks, lo, hi):
    def spec(part):
        return pl.BlockSpec(
            (1, 4, 128, 128),
            lambda s, t, c, n: (t[(s % 2) * 16 + (s // 2 + lo) * 2 + part], 0, 0, 0),
        )

    return pl.pallas_call(
        functools.partial(turn_kernel, lo),
        out_shape=jax.ShapeDtypeStruct((1024, (hi - lo) * 512), BF16),
        grid_spec=pltpu.PrefetchScalarGridSpec(
            num_scalar_prefetch=3,
            grid=((hi - lo) * 2,),
            in_specs=[spec(0), spec(1)],
            out_specs=pl.BlockSpec((1024, 256), lambda s, t, c, n: (0, s)),
        ),
        compiler_params=pltpu.CompilerParams(vmem_limit_bytes=12 << 20),
    )(*lists, blocks, blocks)


def sums_kernel(start, crossed, table, cols, count, first, second, *refs):
    pieces, rest = refs[:ROWS], refs[ROWS:]
    out, sources, dense = rest[-3:]
    step = pl.program_id(0)

    @pl.when(step == 0)
    def _():
        for d in range(ROWS):
            sources[d * 128 : d * 128 + 128, :] = pieces[d][...]

    dense[...] = jnp.zeros_like(dense)
    for part, blocks in enumerate((first, second)):
        row = table[start + step * 2 + part]
        for slot in range(4):
            @pl.when(slot < count[row])
            def _():
                at = pl.multiple_of(cols[row * 4 + slot] * 128, 128)
                dense[part * 128 : part * 128 + 128, pl.ds(at, 128)] = blocks[0, slot]
    value = jnp.dot(dense[...], sources[...], preferred_element_type=F32)
    if crossed:
        value = value + rest[0][...].astype(F32)
    out[...] = value.astype(out.dtype)


def sums(lists, blocks, pieces, side, lo, hi, crossed=None):
    start = side * 16 + lo * 2

    def spec(part):
        return pl.BlockSpec((1, 4, 128, 128), lambda s, t, c, n: (t[start + s * 2 + part], 0, 0, 0))

    line = pl.BlockSpec((256, 768), lambda s, t, c, n: (s, 0))
    whole = pl.BlockSpec((128, 768), lambda s, t, c, n: (0, 0))
    added = [] if crossed is None else [crossed]
    return pl.pallas_call(
        functools.partial(sums_kernel, start, crossed is not None),
        out_shape=jax.ShapeDtypeStruct(((hi - lo) * 256, 768), BF16 if crossed is None else F32),
        grid_spec=pltpu.PrefetchScalarGridSpec(
            num_scalar_prefetch=3,
            grid=(hi - lo,),
            in_specs=[spec(0), spec(1)] + [whole] * ROWS + [line] * len(added),
            out_specs=line,
            scratch_shapes=[pltpu.VMEM((1024, 768), BF16), pltpu.VMEM((256, 1024), BF16)],
        ),
        compiler_params=pltpu.CompilerParams(vmem_limit_bytes=12 << 20),
    )(*lists, blocks, blocks, *pieces, *added)


VM = pl.BlockSpec(memory_space=pltpu.VMEM)


def stack(parts, held):
    at = 0
    for part in parts:
        held[at : at + part.shape[0], :] = part[...]
        at += part.shape[0]
    return at


def spread_kernel(n, turned, *refs):
    parts, out, held = refs[:n], refs[-2], refs[-1]

    @pl.when(pl.program_id(0) == 0)
    def _():
        stack(parts, held)

    out[...] = jnp.dot(turned[...], held[...], preferred_element_type=F32)


def spread(turned, parts):
    width = sum(p.shape[0] for p in parts)
    return pl.pallas_call(
        functools.partial(spread_kernel, len(parts)),
        out_shape=jax.ShapeDtypeStruct((1024, 768), F32),
        grid=(4,),
        in_specs=[pl.BlockSpec((256, width), lambda d: (d, 0))] + [VM] * len(parts),
        out_specs=pl.BlockSpec((256, 768), lambda d: (d, 0)),
        scratch_shapes=[pltpu.VMEM((width, 768), BF16)],
        compiler_params=pltpu.CompilerParams(vmem_limit_bytes=16 << 20),
    )(turned, *parts)


def last_kernel(n, place, turned, before, extra, *refs):
    parts, out, held = refs[:n], refs[-2], refs[-1]
    step = pl.program_id(0)

    @pl.when(step == 0)
    def _():
        stack(parts, held)
        for d in range(ROWS):
            out[d, 128:, :] = extra[...]

    value = jnp.dot(turned[...], held[...], preferred_element_type=F32) + before[...]
    for d in range(2):
        out[place[step * 2 + d], :128, :] = value[d * 128 : d * 128 + 128].astype(BF16)


def last_spread(place, turned, parts, before, extra):
    width = sum(p.shape[0] for p in parts)
    lines = [pl.BlockSpec((256, width), lambda d: (d, 0)), pl.BlockSpec((256, 768), lambda d: (d, 0))]
    shape = (ROWS, 128 + extra.shape[0], 768)
    return pl.pallas_call(
        functools.partial(last_kernel, len(parts)),
        out_shape=jax.ShapeDtypeStruct(shape, BF16),
        grid=(4,),
        in_specs=[pl.BlockSpec(memory_space=pltpu.SMEM)] + lines + [VM] * (1 + len(parts)),
        out_specs=pl.BlockSpec(shape, lambda d: (0, 0, 0)),
        scratch_shapes=[pltpu.VMEM((width, 768), BF16)],
        compiler_params=pltpu.CompilerParams(vmem_limit_bytes=20 << 20),
    )(place, turned, before, extra, *parts)


def silu_slope(hidden):
    sigmoid_value = jax.nn.sigmoid(hidden)
    return sigmoid_value * (1.0 + hidden * (1.0 - sigmoid_value))


def dot(a, b):
    return jnp.dot(a, b, preferred_element_type=F32)


def per_device(features, cotangent, w_self, w_neigh, degree, block_cols, block_count, blocks):
    row, col = lax.axis_index("row"), lax.axis_index("col")
    core, ring, far = col % 2, (col // 2) % RING, col // 16
    offsets = jnp.array(OFFSETS, jnp.int32)
    ring_at = (ring + offsets) % RING
    core_at = jnp.arange(2, dtype=jnp.int32) ^ core
    far_at = jnp.arange(2, dtype=jnp.int32) ^ far
    table = (
        far_at[None, None, :] * 16 + ring_at[None, :, None] * 2 + core_at[:, None, None]
    ).reshape(-1)
    lists = (table, (block_cols[0, 0] ^ row).reshape(-1), block_count[0, 0])
    tile_blocks = blocks[0, 0]
    degree_f = degree.astype(F32)[:, None]
    pieces = [features] + [None] * 7
    for d in (1, 2, 6, 4):
        pieces[d] = to_row(features, d)
    for d in (2, 6, 4):
        pieces[d ^ 1] = to_row(pieces[1], d)
    self_part = dot(features, w_self)
    pieces, self_part = lax.optimization_barrier((pieces, self_part))

    sent = sums(lists, tile_blocks, pieces, 1, 0, 1)
    got = to_partner(sent)
    sent, pieces = lax.optimization_barrier((sent, pieces))
    sent2 = sums(lists, tile_blocks, pieces, 1, 1, 3)
    got2 = to_partner(sent2)
    sent2, pieces = lax.optimization_barrier((sent2, pieces))
    far4 = sums(lists, tile_blocks, pieces, 0, 0, 1, got)
    up, down, pieces = lax.optimization_barrier(
        (far4[:128].astype(BF16), far4[128:].astype(BF16), pieces)
    )
    up, down = along(up, 1), along(down, -1)
    near3 = sums(lists, tile_blocks, pieces, 0, 1, 3, got2)
    near3, pieces = lax.optimization_barrier((near3, pieces))
    sent3 = sums(lists, tile_blocks, pieces, 1, 3, 5)
    got3 = to_partner(sent3)
    up = jnp.concatenate([near3[:128] + up.astype(F32), near3[128:256]], axis=0).astype(BF16)
    down = jnp.concatenate([near3[256:384], near3[384:] + down.astype(F32)], axis=0).astype(BF16)
    up, down, sent3, pieces = lax.optimization_barrier((up, down, sent3, pieces))
    up, down = along(up, 1), along(down, -1)
    sent4 = sums(lists, tile_blocks, pieces, 1, 5, 8)
    got4 = to_partner(sent4)
    sent4, pieces = lax.optimization_barrier((sent4, pieces))
    near2 = sums(lists, tile_blocks, pieces, 0, 3, 5, got3)
    up = (near2[:256] + up.astype(F32)).astype(BF16)
    down = (near2[256:] + down.astype(F32)).astype(BF16)
    up, down, pieces, lists = lax.optimization_barrier((up, down, pieces, lists))
    up, down = along(up, 1), along(down, -1)
    turned_late = turn(lists, tile_blocks, 0, 3)
    near = sums(lists, tile_blocks, pieces, 0, 5, 8, got4)
    up = (near[:256] + up.astype(F32)).astype(BF16)
    down = (near[256:512] + down.astype(F32)).astype(BF16)
    up, down, near, lists, turned_late = lax.optimization_barrier((up, down, near, lists, turned_late))
    up, down = along(up, 1), along(down, -1)
    turned = turn(lists, tile_blocks, 3, 8)
    up, down, turned = lax.optimization_barrier((up, down, turned))
    ends = near[512:] + up.astype(F32) + down.astype(F32)
    summed = ends[:128] + to_far(ends[128:].astype(BF16)).astype(F32)

    aggregate = (summed / degree_f).astype(BF16)
    hidden = self_part + dot(aggregate, w_neigh)
    output = jax.nn.silu(hidden).astype(BF16)
    slope = cotangent.astype(F32) * silu_slope(hidden)
    hidden_grad = slope.astype(BF16)
    shared = (slope / degree_f).astype(BF16)

    across = (((0,), (0,)), ((), ()))
    kept = jnp.where(core == 0, features, aggregate)
    given = jnp.where(core == 0, aggregate, features)
    given = lax.dot_general(given, hidden_grad, across, preferred_element_type=F32).astype(BF16)
    far_shared = to_far(shared)
    pair = lax.dot_general(kept, hidden_grad, across, preferred_element_type=F32)
    shared, given, pair = lax.optimization_barrier(
        (jnp.concatenate([shared, far_shared], axis=0), given, pair)
    )

    held, there = {0: (shared,)}, {}
    given = to_partner(given)
    up, down = along(shared, 1), along(shared, -1)
    up, down, given = lax.optimization_barrier((up, down, given))
    held[7], held[1] = (up,), (down,)
    pair = (pair + given.astype(F32)).astype(BF16)
    part = lax.all_to_all(pair.reshape(ROWS, 96, 768), "row", 0, 0, tiled=True)
    up, down = along(up, 1), along(down, -1)
    held[6], held[2] = (up,), (down,)
    for o in (0, 7, 1, 6, 2):
        there[o] = tuple(to_partner(p) for p in held[o])
    before = spread(turned, [p for o in OFFSETS[3:] for p in held[o] + there[o]])
    up, down = along(up, 1), along(down, -1)
    part = jnp.sum(part.astype(F32), axis=0).astype(BF16)
    part = lax.all_to_all(
        part.reshape(16, 6, 768), "col", 0, 0, axis_index_groups=column_groups(), tiled=True
    )
    up, down, part, before = lax.optimization_barrier((up, down, part, before))
    held[5], held[3] = (up,), (down,)
    held[4] = (along(up[:128], 1), along(down[128:], -1))
    for o in (5, 3):
        there[o] = tuple(to_partner(p) for p in held[o])
    held[4], there[5], there[3] = lax.optimization_barrier((held[4], there[5], there[3]))
    there[4] = tuple(to_partner(p) for p in held[4])
    grad_scale = float(128 * ROWS * COLS) ** (-0.5)
    part = (jnp.sum(part.astype(F32), axis=0) * grad_scale).astype(BF16)
    part = lax.all_to_all(
        jnp.broadcast_to(part[None], (16, 6, 768)), "col", 0, 0, axis_index_groups=column_groups(), tiled=True
    ).reshape(96, 768)
    place = jnp.arange(ROWS, dtype=jnp.int32) ^ row
    mixed = last_spread(place, turned_late, [p for o in OFFSETS[:3] for p in held[o] + there[o]], before, part)
    mixed = lax.all_to_all(mixed, "row", 0, 0, tiled=True)
    full = mixed[:, 128:].reshape(768, 768)
    other = to_partner(full)
    grad_w_self = jnp.where(core == 0, full, other).astype(F32)
    grad_w_neigh = jnp.where(core == 0, other, full).astype(F32)
    back = jnp.sum(mixed[:, :128].astype(F32), axis=0)
    against = (((1,), (1,)), ((), ()))
    grad_features = (
        lax.dot_general(hidden_grad, w_self, against, preferred_element_type=F32)
        + lax.dot_general(back.astype(BF16), w_neigh, against, preferred_element_type=F32)
    ).astype(BF16)
    return (output, grad_features, grad_w_self, grad_w_neigh)


def solution(mesh):
    placed = (
        P(("row", "col"), None),
        P(("row", "col"), None),
        P(),
        P(),
        P(("row", "col")),
        P("row", "col", None, None),
        P("row", "col", None),
        P("row", "col", None, None, None, None),
    )
    return jax.shard_map(
        per_device,
        mesh=mesh,
        in_specs=placed,
        out_specs=(P(("row", "col"), None), P(("row", "col"), None), P(), P()),
        check_vma=False,
    )
```

```python
import functools

import jax
import jax.numpy as jnp
from jax import lax
from jax.experimental import pallas as pl
from jax.experimental.pallas import tpu as pltpu
from jax.sharding import PartitionSpec as P

ROWS, COLS, RING = 8, 32, 8
OFFSETS = (4, 3, 5, 2, 6, 1, 7, 0)
F32, BF16 = jnp.float32, jnp.bfloat16


def to_partner(value):
    return lax.ppermute(value, "col", [(j, j ^ 1) for j in range(COLS)])


def to_far(value):
    return lax.ppermute(value, "col", [(j, j ^ 16) for j in range(COLS)])


def along(value, step):
    pairs = [(j, (j & 17) | (((j // 2 + step) % RING) * 2)) for j in range(COLS)]
    return lax.ppermute(value, "col", pairs)


def to_row(value, flip):
    return lax.ppermute(value, "row", [(i, i ^ flip) for i in range(ROWS)])


def column_groups():
    return [[c for c in range(COLS) if c % 2 == k] for k in range(2)]


def turn_kernel(lo, table, cols, count, first, second, turned):
    step = pl.program_id(0) + lo * 2
    turned[...] = jnp.zeros_like(turned)
    for part, blocks in enumerate((first, second)):
        row = table[(step % 2) * 16 + (step // 2) * 2 + part]
        for slot in range(4):
            @pl.when(slot < count[row])
            def _():
                at = pl.multiple_of(cols[row * 4 + slot] * 128, 128)
                turned[pl.ds(at, 128), part * 128 : part * 128 + 128] = blocks[0, slot].T


def turn(lists, blocks, lo, hi):
    def spec(part):
        return pl.BlockSpec(
            (1, 4, 128, 128),
            lambda s, t, c, n: (t[(s % 2) * 16 + (s // 2 + lo) * 2 + part], 0, 0, 0),
        )

    return pl.pallas_call(
        functools.partial(turn_kernel, lo),
        out_shape=jax.ShapeDtypeStruct((1024, (hi - lo) * 512), BF16),
        grid_spec=pltpu.PrefetchScalarGridSpec(
            num_scalar_prefetch=3,
            grid=((hi - lo) * 2,),
            in_specs=[spec(0), spec(1)],
            out_specs=pl.BlockSpec((1024, 256), lambda s, t, c, n: (0, s)),
        ),
        compiler_params=pltpu.CompilerParams(vmem_limit_bytes=12 << 20),
    )(*lists, blocks, blocks)


def sums_kernel(start, crossed, table, cols, count, first, second, *refs):
    pieces, rest = refs[:ROWS], refs[ROWS:]
    out, sources, dense = rest[-3:]
    step = pl.program_id(0)

    @pl.when(step == 0)
    def _():
        for d in range(ROWS):
            sources[d * 128 : d * 128 + 128, :] = pieces[d][...]

    dense[...] = jnp.zeros_like(dense)
    for part, blocks in enumerate((first, second)):
        row = table[start + step * 2 + part]
        for slot in range(4):
            @pl.when(slot < count[row])
            def _():
                at = pl.multiple_of(cols[row * 4 + slot] * 128, 128)
                dense[part * 128 : part * 128 + 128, pl.ds(at, 128)] = blocks[0, slot]
    value = jnp.dot(dense[...], sources[...], preferred_element_type=F32)
    if crossed:
        value = value + rest[0][...].astype(F32)
    out[...] = value.astype(out.dtype)


def sums(lists, blocks, pieces, side, lo, hi, crossed=None):
    start = side * 16 + lo * 2

    def spec(part):
        return pl.BlockSpec((1, 4, 128, 128), lambda s, t, c, n: (t[start + s * 2 + part], 0, 0, 0))

    line = pl.BlockSpec((256, 768), lambda s, t, c, n: (s, 0))
    whole = pl.BlockSpec((128, 768), lambda s, t, c, n: (0, 0))
    added = [] if crossed is None else [crossed]
    return pl.pallas_call(
        functools.partial(sums_kernel, start, crossed is not None),
        out_shape=jax.ShapeDtypeStruct(((hi - lo) * 256, 768), BF16 if crossed is None else F32),
        grid_spec=pltpu.PrefetchScalarGridSpec(
            num_scalar_prefetch=3,
            grid=(hi - lo,),
            in_specs=[spec(0), spec(1)] + [whole] * ROWS + [line] * len(added),
            out_specs=line,
            scratch_shapes=[pltpu.VMEM((1024, 768), BF16), pltpu.VMEM((256, 1024), BF16)],
        ),
        compiler_params=pltpu.CompilerParams(vmem_limit_bytes=12 << 20),
    )(*lists, blocks, blocks, *pieces, *added)


VM = pl.BlockSpec(memory_space=pltpu.VMEM)


def stack(parts, held):
    at = 0
    for part in parts:
        held[at : at + part.shape[0], :] = part[...]
        at += part.shape[0]
    return at


def spread_kernel(n, turned, *refs):
    parts, out, held = refs[:n], refs[-2], refs[-1]

    @pl.when(pl.program_id(0) == 0)
    def _():
        stack(parts, held)

    out[...] = jnp.dot(turned[...], held[...], preferred_element_type=F32)


def spread(turned, parts):
    width = sum(p.shape[0] for p in parts)
    return pl.pallas_call(
        functools.partial(spread_kernel, len(parts)),
        out_shape=jax.ShapeDtypeStruct((1024, 768), F32),
        grid=(4,),
        in_specs=[pl.BlockSpec((256, width), lambda d: (d, 0))] + [VM] * len(parts),
        out_specs=pl.BlockSpec((256, 768), lambda d: (d, 0)),
        scratch_shapes=[pltpu.VMEM((width, 768), BF16)],
        compiler_params=pltpu.CompilerParams(vmem_limit_bytes=16 << 20),
    )(turned, *parts)


def last_kernel(n, place, turned, before, *refs):
    parts, out, held = refs[:n], refs[-2], refs[-1]
    step = pl.program_id(0)

    @pl.when(step == 0)
    def _():
        stack(parts, held)

    value = jnp.dot(turned[...], held[...], preferred_element_type=F32) + before[...]
    for d in range(2):
        out[place[step * 2 + d], :128, :] = value[d * 128 : d * 128 + 128].astype(BF16)


def last_spread(place, turned, parts, before):
    width = sum(p.shape[0] for p in parts)
    lines = [pl.BlockSpec((256, width), lambda d: (d, 0)), pl.BlockSpec((256, 768), lambda d: (d, 0))]
    shape = (ROWS, 224, 768)
    return pl.pallas_call(
        functools.partial(last_kernel, len(parts)),
        out_shape=jax.ShapeDtypeStruct(shape, BF16),
        grid=(4,),
        in_specs=[pl.BlockSpec(memory_space=pltpu.SMEM)] + lines + [VM] * len(parts),
        out_specs=pl.BlockSpec(shape, lambda d: (0, 0, 0)),
        scratch_shapes=[pltpu.VMEM((width, 768), BF16)],
        compiler_params=pltpu.CompilerParams(vmem_limit_bytes=20 << 20),
    )(place, turned, before, *parts)


def fill_kernel(extra, mixed, out):
    for d in range(ROWS):
        out[d] = extra[...]


def fill(mixed, extra):
    return pl.pallas_call(
        fill_kernel,
        out_shape=jax.ShapeDtypeStruct(mixed.shape, BF16),
        grid=(3,),
        in_specs=[
            pl.BlockSpec((32, 768), lambda k: (k, 0)),
            pl.BlockSpec(memory_space=pl.ANY),
        ],
        out_specs=pl.BlockSpec((ROWS, 32, 768), lambda k: (0, 4 + k, 0)),
        input_output_aliases={1: 0},
        compiler_params=pltpu.CompilerParams(vmem_limit_bytes=8 << 20),
    )(extra, mixed)


def silu_slope(hidden):
    sigmoid_value = jax.nn.sigmoid(hidden)
    return sigmoid_value * (1.0 + hidden * (1.0 - sigmoid_value))


def dot(a, b):
    return jnp.dot(a, b, preferred_element_type=F32)


def per_device(features, cotangent, w_self, w_neigh, degree, block_cols, block_count, blocks):
    row, col = lax.axis_index("row"), lax.axis_index("col")
    core, ring, far = col % 2, (col // 2) % RING, col // 16
    offsets = jnp.array(OFFSETS, jnp.int32)
    ring_at = (ring + offsets) % RING
    core_at = jnp.arange(2, dtype=jnp.int32) ^ core
    far_at = jnp.arange(2, dtype=jnp.int32) ^ far
    table = (
        far_at[None, None, :] * 16 + ring_at[None, :, None] * 2 + core_at[:, None, None]
    ).reshape(-1)
    lists = (table, (block_cols[0, 0] ^ row).reshape(-1), block_count[0, 0])
    tile_blocks = blocks[0, 0]
    degree_f = degree.astype(F32)[:, None]
    pieces = [features] + [None] * 7
    for d in (1, 2, 6, 4):
        pieces[d] = to_row(features, d)
    for d in (2, 6, 4):
        pieces[d ^ 1] = to_row(pieces[1], d)
    self_part = dot(features, w_self)
    pieces, self_part = lax.optimization_barrier((pieces, self_part))

    sent = sums(lists, tile_blocks, pieces, 1, 0, 1)
    got = to_partner(sent)
    sent, pieces = lax.optimization_barrier((sent, pieces))
    sent2 = sums(lists, tile_blocks, pieces, 1, 1, 3)
    got2 = to_partner(sent2)
    sent2, pieces = lax.optimization_barrier((sent2, pieces))
    far4 = sums(lists, tile_blocks, pieces, 0, 0, 1, got)
    up, down, pieces = lax.optimization_barrier(
        (far4[:128].astype(BF16), far4[128:].astype(BF16), pieces)
    )
    up, down = along(up, 1), along(down, -1)
    near3 = sums(lists, tile_blocks, pieces, 0, 1, 3, got2)
    near3, pieces = lax.optimization_barrier((near3, pieces))
    sent3 = sums(lists, tile_blocks, pieces, 1, 3, 5)
    got3 = to_partner(sent3)
    up = jnp.concatenate([near3[:128] + up.astype(F32), near3[128:256]], axis=0).astype(BF16)
    down = jnp.concatenate([near3[256:384], near3[384:] + down.astype(F32)], axis=0).astype(BF16)
    up, down, sent3, pieces = lax.optimization_barrier((up, down, sent3, pieces))
    up, down = along(up, 1), along(down, -1)
    sent4 = sums(lists, tile_blocks, pieces, 1, 5, 8)
    got4 = to_partner(sent4)
    sent4, pieces = lax.optimization_barrier((sent4, pieces))
    near2 = sums(lists, tile_blocks, pieces, 0, 3, 5, got3)
    up = (near2[:256] + up.astype(F32)).astype(BF16)
    down = (near2[256:] + down.astype(F32)).astype(BF16)
    up, down, pieces, lists = lax.optimization_barrier((up, down, pieces, lists))
    up, down = along(up, 1), along(down, -1)
    turned_late = turn(lists, tile_blocks, 0, 3)
    near = sums(lists, tile_blocks, pieces, 0, 5, 8, got4)
    up = (near[:256] + up.astype(F32)).astype(BF16)
    down = (near[256:512] + down.astype(F32)).astype(BF16)
    up, down, near, lists, turned_late = lax.optimization_barrier((up, down, near, lists, turned_late))
    up, down = along(up, 1), along(down, -1)
    turned = turn(lists, tile_blocks, 3, 8)
    up, down, turned = lax.optimization_barrier((up, down, turned))
    ends = near[512:] + up.astype(F32) + down.astype(F32)
    summed = ends[:128] + to_far(ends[128:].astype(BF16)).astype(F32)

    aggregate = (summed / degree_f).astype(BF16)
    hidden = self_part + dot(aggregate, w_neigh)
    output = jax.nn.silu(hidden).astype(BF16)
    slope = cotangent.astype(F32) * silu_slope(hidden)
    hidden_grad = slope.astype(BF16)
    shared = (slope / degree_f).astype(BF16)

    across = (((0,), (0,)), ((), ()))
    kept = jnp.where(core == 0, features, aggregate)
    given = jnp.where(core == 0, aggregate, features)
    given = lax.dot_general(given, hidden_grad, across, preferred_element_type=F32).astype(BF16)
    far_shared = to_far(shared)
    pair = lax.dot_general(kept, hidden_grad, across, preferred_element_type=F32)
    shared, given, pair = lax.optimization_barrier(
        (jnp.concatenate([shared, far_shared], axis=0), given, pair)
    )

    held, there = {0: (shared,)}, {}
    pair = (pair + to_partner(given).astype(F32)).astype(BF16)
    part = lax.psum_scatter(pair, "row", scatter_dimension=0, tiled=True)
    up, down = along(shared, 1), along(shared, -1)
    held[7], held[1] = (up,), (down,)
    up, down = along(up, 1), along(down, -1)
    held[6], held[2] = (up,), (down,)
    for o in (0, 7, 1, 6, 2):
        there[o] = tuple(to_partner(p) for p in held[o])
    before = spread(turned, [p for o in OFFSETS[3:] for p in held[o] + there[o]])
    up, down = along(up, 1), along(down, -1)
    up, down, before = lax.optimization_barrier((up, down, before))
    held[5], held[3] = (up,), (down,)
    held[4] = (along(up[:128], 1), along(down[128:], -1))
    for o in (5, 3):
        there[o] = tuple(to_partner(p) for p in held[o])
    held[4], there[5], there[3] = lax.optimization_barrier((held[4], there[5], there[3]))
    there[4] = tuple(to_partner(p) for p in held[4])
    place = jnp.arange(ROWS, dtype=jnp.int32) ^ row
    mixed = last_spread(place, turned_late, [p for o in OFFSETS[:3] for p in held[o] + there[o]], before)
    mixed, part = lax.optimization_barrier((mixed, part))

    part = lax.all_to_all(
        part.reshape(16, 6, 768), "col", 0, 0, axis_index_groups=column_groups(), tiled=True
    )
    grad_scale = float(128 * ROWS * COLS) ** (-0.5)
    part = (jnp.sum(part.astype(F32), axis=0) * grad_scale).astype(BF16)
    part = lax.all_to_all(
        jnp.broadcast_to(part[None], (16, 6, 768)), "col", 0, 0, axis_index_groups=column_groups(), tiled=True
    ).reshape(96, 768)
    mixed = lax.all_to_all(fill(mixed, part), "row", 0, 0, tiled=True)
    full = mixed[:, 128:].reshape(768, 768)
    other = to_partner(full)
    grad_w_self = jnp.where(core == 0, full, other).astype(F32)
    grad_w_neigh = jnp.where(core == 0, other, full).astype(F32)
    back = jnp.sum(mixed[:, :128].astype(F32), axis=0)
    against = (((1,), (1,)), ((), ()))
    grad_features = (
        lax.dot_general(hidden_grad, w_self, against, preferred_element_type=F32)
        + lax.dot_general(back.astype(BF16), w_neigh, against, preferred_element_type=F32)
    ).astype(BF16)
    return (output, grad_features, grad_w_self, grad_w_neigh)


def solution(mesh):
    placed = (
        P(("row", "col"), None),
        P(("row", "col"), None),
        P(),
        P(),
        P(("row", "col")),
        P("row", "col", None, None),
        P("row", "col", None),
        P("row", "col", None, None, None, None),
    )
    return jax.shard_map(
        per_device,
        mesh=mesh,
        in_specs=placed,
        out_specs=(P(("row", "col"), None), P(("row", "col"), None), P(), P()),
        check_vma=False,
    )
```

```python
import functools

import jax
import jax.numpy as jnp
from jax import lax
from jax.experimental import pallas as pl
from jax.experimental.pallas import tpu as pltpu
from jax.sharding import PartitionSpec as P

ROWS, COLS, RING = 8, 32, 8
OFFSETS = (4, 3, 5, 2, 6, 1, 7, 0)
F32, BF16 = jnp.float32, jnp.bfloat16


def to_partner(value):
    return lax.ppermute(value, "col", [(j, j ^ 1) for j in range(COLS)])


def to_far(value):
    return lax.ppermute(value, "col", [(j, j ^ 16) for j in range(COLS)])


def along(value, step):
    pairs = [(j, (j & 17) | (((j // 2 + step) % RING) * 2)) for j in range(COLS)]
    return lax.ppermute(value, "col", pairs)


def to_row(value, flip):
    return lax.ppermute(value, "row", [(i, i ^ flip) for i in range(ROWS)])


def column_groups():
    return [[c for c in range(COLS) if c % 2 == k] for k in range(2)]


def turn_kernel(lo, table, cols, count, first, second, turned):
    step = pl.program_id(0) + lo * 2
    turned[...] = jnp.zeros_like(turned)
    for part, blocks in enumerate((first, second)):
        row = table[(step % 2) * 16 + (step // 2) * 2 + part]
        for slot in range(4):
            @pl.when(slot < count[row])
            def _():
                at = pl.multiple_of(cols[row * 4 + slot] * 128, 128)
                turned[pl.ds(at, 128), part * 128 : part * 128 + 128] = blocks[0, slot].T


def turn(lists, blocks, lo, hi):
    def spec(part):
        return pl.BlockSpec(
            (1, 4, 128, 128),
            lambda s, t, c, n: (t[(s % 2) * 16 + (s // 2 + lo) * 2 + part], 0, 0, 0),
        )

    return pl.pallas_call(
        functools.partial(turn_kernel, lo),
        out_shape=jax.ShapeDtypeStruct((1024, (hi - lo) * 512), BF16),
        grid_spec=pltpu.PrefetchScalarGridSpec(
            num_scalar_prefetch=3,
            grid=((hi - lo) * 2,),
            in_specs=[spec(0), spec(1)],
            out_specs=pl.BlockSpec((1024, 256), lambda s, t, c, n: (0, s)),
        ),
        compiler_params=pltpu.CompilerParams(vmem_limit_bytes=12 << 20),
    )(*lists, blocks, blocks)


def sums_kernel(start, crossed, table, cols, count, first, second, *refs):
    pieces, rest = refs[:ROWS], refs[ROWS:]
    out, sources, dense = rest[-3:]
    step = pl.program_id(0)

    @pl.when(step == 0)
    def _():
        for d in range(ROWS):
            sources[d * 128 : d * 128 + 128, :] = pieces[d][...]

    dense[...] = jnp.zeros_like(dense)
    for part, blocks in enumerate((first, second)):
        row = table[start + step * 2 + part]
        for slot in range(4):
            @pl.when(slot < count[row])
            def _():
                at = pl.multiple_of(cols[row * 4 + slot] * 128, 128)
                dense[part * 128 : part * 128 + 128, pl.ds(at, 128)] = blocks[0, slot]
    value = jnp.dot(dense[...], sources[...], preferred_element_type=F32)
    if crossed:
        value = value + rest[0][...].astype(F32)
    out[...] = value.astype(out.dtype)


def sums(lists, blocks, pieces, side, lo, hi, crossed=None):
    start = side * 16 + lo * 2

    def spec(part):
        return pl.BlockSpec((1, 4, 128, 128), lambda s, t, c, n: (t[start + s * 2 + part], 0, 0, 0))

    line = pl.BlockSpec((256, 768), lambda s, t, c, n: (s, 0))
    whole = pl.BlockSpec((128, 768), lambda s, t, c, n: (0, 0))
    added = [] if crossed is None else [crossed]
    return pl.pallas_call(
        functools.partial(sums_kernel, start, crossed is not None),
        out_shape=jax.ShapeDtypeStruct(((hi - lo) * 256, 768), BF16 if crossed is None else F32),
        grid_spec=pltpu.PrefetchScalarGridSpec(
            num_scalar_prefetch=3,
            grid=(hi - lo,),
            in_specs=[spec(0), spec(1)] + [whole] * ROWS + [line] * len(added),
            out_specs=line,
            scratch_shapes=[pltpu.VMEM((1024, 768), BF16), pltpu.VMEM((256, 1024), BF16)],
        ),
        compiler_params=pltpu.CompilerParams(vmem_limit_bytes=12 << 20),
    )(*lists, blocks, blocks, *pieces, *added)


VM = pl.BlockSpec(memory_space=pltpu.VMEM)


def stack(parts, held):
    at = 0
    for part in parts:
        held[at : at + part.shape[0], :] = part[...]
        at += part.shape[0]
    return at


def spread_kernel(n, turned, *refs):
    parts, out, held = refs[:n], refs[-2], refs[-1]

    @pl.when(pl.program_id(0) == 0)
    def _():
        stack(parts, held)

    out[...] = jnp.dot(turned[...], held[...], preferred_element_type=F32)


def spread(turned, parts):
    width = sum(p.shape[0] for p in parts)
    return pl.pallas_call(
        functools.partial(spread_kernel, len(parts)),
        out_shape=jax.ShapeDtypeStruct((1024, 768), F32),
        grid=(4,),
        in_specs=[pl.BlockSpec((256, width), lambda d: (d, 0))] + [VM] * len(parts),
        out_specs=pl.BlockSpec((256, 768), lambda d: (d, 0)),
        scratch_shapes=[pltpu.VMEM((width, 768), BF16)],
        compiler_params=pltpu.CompilerParams(vmem_limit_bytes=16 << 20),
    )(turned, *parts)


def last_kernel(n, turned, before, *refs):
    parts, outs, held = refs[:n], refs[n:-1], refs[-1]
    stack(parts, held)
    for d in range(ROWS):
        rows = slice(d * 128, d * 128 + 128)
        value = jnp.dot(turned[rows, :], held[...], preferred_element_type=F32) + before[rows, :]
        outs[d][...] = value.astype(outs[d].dtype)


def last_spread(turned, parts, before):
    width = sum(p.shape[0] for p in parts)
    return pl.pallas_call(
        functools.partial(last_kernel, len(parts)),
        out_shape=[jax.ShapeDtypeStruct((128, 768), BF16 if d else F32) for d in range(ROWS)],
        in_specs=[VM] * (2 + len(parts)),
        out_specs=[VM] * ROWS,
        scratch_shapes=[pltpu.VMEM((width, 768), BF16)],
        compiler_params=pltpu.CompilerParams(vmem_limit_bytes=20 << 20),
    )(turned, before, *parts)


def silu_slope(hidden):
    sigmoid_value = jax.nn.sigmoid(hidden)
    return sigmoid_value * (1.0 + hidden * (1.0 - sigmoid_value))


def dot(a, b):
    return jnp.dot(a, b, preferred_element_type=F32)


def per_device(features, cotangent, w_self, w_neigh, degree, block_cols, block_count, blocks):
    row, col = lax.axis_index("row"), lax.axis_index("col")
    core, ring, far = col % 2, (col // 2) % RING, col // 16
    offsets = jnp.array(OFFSETS, jnp.int32)
    ring_at = (ring + offsets) % RING
    core_at = jnp.arange(2, dtype=jnp.int32) ^ core
    far_at = jnp.arange(2, dtype=jnp.int32) ^ far
    table = (
        far_at[None, None, :] * 16 + ring_at[None, :, None] * 2 + core_at[:, None, None]
    ).reshape(-1)
    lists = (table, (block_cols[0, 0] ^ row).reshape(-1), block_count[0, 0])
    tile_blocks = blocks[0, 0]
    degree_f = degree.astype(F32)[:, None]
    pieces = [features] + [None] * 7
    for d in (1, 2, 6, 4):
        pieces[d] = to_row(features, d)
    for d in (2, 6, 4):
        pieces[d ^ 1] = to_row(pieces[1], d)
    self_part = dot(features, w_self)
    pieces, self_part = lax.optimization_barrier((pieces, self_part))

    sent = sums(lists, tile_blocks, pieces, 1, 0, 1)
    got = to_partner(sent)
    sent, pieces = lax.optimization_barrier((sent, pieces))
    sent2 = sums(lists, tile_blocks, pieces, 1, 1, 3)
    got2 = to_partner(sent2)
    sent2, pieces = lax.optimization_barrier((sent2, pieces))
    far4 = sums(lists, tile_blocks, pieces, 0, 0, 1, got)
    up, down, pieces = lax.optimization_barrier(
        (far4[:128].astype(BF16), far4[128:].astype(BF16), pieces)
    )
    up, down = along(up, 1), along(down, -1)
    near3 = sums(lists, tile_blocks, pieces, 0, 1, 3, got2)
    near3, pieces = lax.optimization_barrier((near3, pieces))
    sent3 = sums(lists, tile_blocks, pieces, 1, 3, 5)
    got3 = to_partner(sent3)
    up = jnp.concatenate([near3[:128] + up.astype(F32), near3[128:256]], axis=0).astype(BF16)
    down = jnp.concatenate([near3[256:384], near3[384:] + down.astype(F32)], axis=0).astype(BF16)
    up, down, sent3, pieces = lax.optimization_barrier((up, down, sent3, pieces))
    up, down = along(up, 1), along(down, -1)
    sent4 = sums(lists, tile_blocks, pieces, 1, 5, 8)
    got4 = to_partner(sent4)
    sent4, pieces = lax.optimization_barrier((sent4, pieces))
    near2 = sums(lists, tile_blocks, pieces, 0, 3, 5, got3)
    up = (near2[:256] + up.astype(F32)).astype(BF16)
    down = (near2[256:] + down.astype(F32)).astype(BF16)
    up, down, pieces, lists = lax.optimization_barrier((up, down, pieces, lists))
    up, down = along(up, 1), along(down, -1)
    turned_late = turn(lists, tile_blocks, 0, 3)
    near = sums(lists, tile_blocks, pieces, 0, 5, 8, got4)
    up = (near[:256] + up.astype(F32)).astype(BF16)
    down = (near[256:512] + down.astype(F32)).astype(BF16)
    up, down, near, lists, turned_late = lax.optimization_barrier((up, down, near, lists, turned_late))
    up, down = along(up, 1), along(down, -1)
    turned = turn(lists, tile_blocks, 3, 8)
    up, down, turned = lax.optimization_barrier((up, down, turned))
    ends = near[512:] + up.astype(F32) + down.astype(F32)
    summed = ends[:128] + to_far(ends[128:].astype(BF16)).astype(F32)

    aggregate = (summed / degree_f).astype(BF16)
    hidden = self_part + dot(aggregate, w_neigh)
    output = jax.nn.silu(hidden).astype(BF16)
    slope = cotangent.astype(F32) * silu_slope(hidden)
    hidden_grad = slope.astype(BF16)
    shared = (slope / degree_f).astype(BF16)

    across = (((0,), (0,)), ((), ()))
    kept = jnp.where(core == 0, features, aggregate)
    given = jnp.where(core == 0, aggregate, features)
    given = lax.dot_general(given, hidden_grad, across, preferred_element_type=F32).astype(BF16)
    far_shared = to_far(shared)
    pair = lax.dot_general(kept, hidden_grad, across, preferred_element_type=F32)
    shared, given, pair = lax.optimization_barrier(
        (jnp.concatenate([shared, far_shared], axis=0), given, pair)
    )

    held, there = {0: (shared,)}, {}
    pair = (pair + to_partner(given).astype(F32)).astype(BF16)
    part = lax.psum_scatter(pair, "row", scatter_dimension=0, tiled=True)
    up, down = along(shared, 1), along(shared, -1)
    held[7], held[1] = (up,), (down,)
    up, down = along(up, 1), along(down, -1)
    held[6], held[2] = (up,), (down,)
    for o in (0, 7, 1, 6, 2):
        there[o] = tuple(to_partner(p) for p in held[o])
    before = spread(turned, [p for o in OFFSETS[3:] for p in held[o] + there[o]])
    up, down = along(up, 1), along(down, -1)
    up, down, before = lax.optimization_barrier((up, down, before))
    held[5], held[3] = (up,), (down,)
    held[4] = (along(up[:128], 1), along(down[128:], -1))
    for o in (5, 3):
        there[o] = tuple(to_partner(p) for p in held[o])
    held[4], there[5], there[3] = lax.optimization_barrier((held[4], there[5], there[3]))
    there[4] = tuple(to_partner(p) for p in held[4])
    chunks = last_spread(turned_late, [p for o in OFFSETS[:3] for p in held[o] + there[o]], before)
    chunks, part = lax.optimization_barrier((chunks, part))

    first = [to_row(chunks[d], d) for d in (2, 6, 1, 4)]
    part = lax.all_to_all(
        part.reshape(16, 6, 768), "col", 0, 0, axis_index_groups=column_groups(), tiled=True
    )
    rest = chunks[3], chunks[5], chunks[7]
    first, rest, part = lax.optimization_barrier((first, rest, part))
    second = [to_row(value, d) for value, d in zip(rest, (3, 5, 7))]
    grad_scale = float(128 * ROWS * COLS) ** (-0.5)
    part = (jnp.sum(part.astype(F32), axis=0) * grad_scale).astype(BF16)
    part = lax.all_to_all(
        jnp.broadcast_to(part[None], (16, 6, 768)), "col", 0, 0, axis_index_groups=column_groups(), tiled=True
    ).reshape(96, 768)
    second, part = lax.optimization_barrier((second, part))
    full = lax.all_to_all(jnp.broadcast_to(part[None], (ROWS, 96, 768)), "row", 0, 0, tiled=True)
    full = full.reshape(768, 768)
    other = to_partner(full)
    grad_w_self = jnp.where(core == 0, full, other).astype(F32)
    grad_w_neigh = jnp.where(core == 0, other, full).astype(F32)
    back = chunks[0]
    for value in first + second:
        back = back + value.astype(F32)
    against = (((1,), (1,)), ((), ()))
    grad_features = (
        lax.dot_general(hidden_grad, w_self, against, preferred_element_type=F32)
        + lax.dot_general(back.astype(BF16), w_neigh, against, preferred_element_type=F32)
    ).astype(BF16)
    return (output, grad_features, grad_w_self, grad_w_neigh)


def solution(mesh):
    placed = (
        P(("row", "col"), None),
        P(("row", "col"), None),
        P(),
        P(),
        P(("row", "col")),
        P("row", "col", None, None),
        P("row", "col", None),
        P("row", "col", None, None, None, None),
    )
    return jax.shard_map(
        per_device,
        mesh=mesh,
        in_specs=placed,
        out_specs=(P(("row", "col"), None), P(("row", "col"), None), P(), P()),
        check_vma=False,
    )
```

```python
import functools

import jax
import jax.numpy as jnp
from jax import lax
from jax.experimental import pallas as pl
from jax.experimental.pallas import tpu as pltpu
from jax.sharding import PartitionSpec as P

ROWS, COLS, RING = 8, 32, 8
OFFSETS = (4, 3, 5, 2, 6, 1, 7, 0)
F32, BF16 = jnp.float32, jnp.bfloat16


def to_partner(value):
    return lax.ppermute(value, "col", [(j, j ^ 1) for j in range(COLS)])


def to_far(value):
    return lax.ppermute(value, "col", [(j, j ^ 16) for j in range(COLS)])


def along(value, step):
    pairs = [(j, (j & 17) | (((j // 2 + step) % RING) * 2)) for j in range(COLS)]
    return lax.ppermute(value, "col", pairs)


def to_row(value, flip):
    return lax.ppermute(value, "row", [(i, i ^ flip) for i in range(ROWS)])


def column_groups():
    return [[c for c in range(COLS) if c % 2 == k] for k in range(2)]


def turn_kernel(lo, table, cols, count, first, second, turned):
    step = pl.program_id(0) + lo * 2
    turned[...] = jnp.zeros_like(turned)
    for part, blocks in enumerate((first, second)):
        row = table[(step % 2) * 16 + (step // 2) * 2 + part]
        for slot in range(4):
            @pl.when(slot < count[row])
            def _():
                at = pl.multiple_of(cols[row * 4 + slot] * 128, 128)
                turned[pl.ds(at, 128), part * 128 : part * 128 + 128] = blocks[0, slot].T


def turn(lists, blocks, lo, hi):
    def spec(part):
        return pl.BlockSpec(
            (1, 4, 128, 128),
            lambda s, t, c, n: (t[(s % 2) * 16 + (s // 2 + lo) * 2 + part], 0, 0, 0),
        )

    return pl.pallas_call(
        functools.partial(turn_kernel, lo),
        out_shape=jax.ShapeDtypeStruct((1024, (hi - lo) * 512), BF16),
        grid_spec=pltpu.PrefetchScalarGridSpec(
            num_scalar_prefetch=3,
            grid=((hi - lo) * 2,),
            in_specs=[spec(0), spec(1)],
            out_specs=pl.BlockSpec((1024, 256), lambda s, t, c, n: (0, s)),
        ),
        compiler_params=pltpu.CompilerParams(vmem_limit_bytes=12 << 20),
    )(*lists, blocks, blocks)


def sums_kernel(start, crossed, table, cols, count, first, second, *refs):
    pieces, rest = refs[:ROWS], refs[ROWS:]
    out, sources, dense = rest[-3:]
    step = pl.program_id(0)

    @pl.when(step == 0)
    def _():
        for d in range(ROWS):
            sources[d * 128 : d * 128 + 128, :] = pieces[d][...]

    dense[...] = jnp.zeros_like(dense)
    for part, blocks in enumerate((first, second)):
        row = table[start + step * 2 + part]
        for slot in range(4):
            @pl.when(slot < count[row])
            def _():
                at = pl.multiple_of(cols[row * 4 + slot] * 128, 128)
                dense[part * 128 : part * 128 + 128, pl.ds(at, 128)] = blocks[0, slot]
    value = jnp.dot(dense[...], sources[...], preferred_element_type=F32)
    if crossed:
        value = value + rest[0][...].astype(F32)
    out[...] = value.astype(out.dtype)


def sums(lists, blocks, pieces, side, lo, hi, crossed=None):
    start = side * 16 + lo * 2

    def spec(part):
        return pl.BlockSpec((1, 4, 128, 128), lambda s, t, c, n: (t[start + s * 2 + part], 0, 0, 0))

    line = pl.BlockSpec((256, 768), lambda s, t, c, n: (s, 0))
    whole = pl.BlockSpec((128, 768), lambda s, t, c, n: (0, 0))
    added = [] if crossed is None else [crossed]
    return pl.pallas_call(
        functools.partial(sums_kernel, start, crossed is not None),
        out_shape=jax.ShapeDtypeStruct(((hi - lo) * 256, 768), BF16 if crossed is None else F32),
        grid_spec=pltpu.PrefetchScalarGridSpec(
            num_scalar_prefetch=3,
            grid=(hi - lo,),
            in_specs=[spec(0), spec(1)] + [whole] * ROWS + [line] * len(added),
            out_specs=line,
            scratch_shapes=[pltpu.VMEM((1024, 768), BF16), pltpu.VMEM((256, 1024), BF16)],
        ),
        compiler_params=pltpu.CompilerParams(vmem_limit_bytes=12 << 20),
    )(*lists, blocks, blocks, *pieces, *added)


VM = pl.BlockSpec(memory_space=pltpu.VMEM)


def stack(parts, held):
    at = 0
    for part in parts:
        held[at : at + part.shape[0], :] = part[...]
        at += part.shape[0]
    return at


def spread_kernel(n, turned, *refs):
    parts, out, held = refs[:n], refs[-2], refs[-1]

    @pl.when(pl.program_id(0) == 0)
    def _():
        stack(parts, held)

    out[...] = jnp.dot(turned[...], held[...], preferred_element_type=F32)


def spread(turned, parts):
    width = sum(p.shape[0] for p in parts)
    return pl.pallas_call(
        functools.partial(spread_kernel, len(parts)),
        out_shape=jax.ShapeDtypeStruct((1024, 768), F32),
        grid=(4,),
        in_specs=[pl.BlockSpec((256, width), lambda d: (d, 0))] + [VM] * len(parts),
        out_specs=pl.BlockSpec((256, 768), lambda d: (d, 0)),
        scratch_shapes=[pltpu.VMEM((width, 768), BF16)],
        compiler_params=pltpu.CompilerParams(vmem_limit_bytes=16 << 20),
    )(turned, *parts)


def last_kernel(n, turned, before, *refs):
    parts, outs, held = refs[:n], refs[n:-1], refs[-1]
    stack(parts, held)
    for d in range(ROWS):
        rows = slice(d * 128, d * 128 + 128)
        value = jnp.dot(turned[rows, :], held[...], preferred_element_type=F32) + before[rows, :]
        outs[d][...] = value.astype(outs[d].dtype)


def last_spread(turned, parts, before):
    width = sum(p.shape[0] for p in parts)
    return pl.pallas_call(
        functools.partial(last_kernel, len(parts)),
        out_shape=[jax.ShapeDtypeStruct((128, 768), BF16 if d else F32) for d in range(ROWS)],
        in_specs=[VM] * (2 + len(parts)),
        out_specs=[VM] * ROWS,
        scratch_shapes=[pltpu.VMEM((width, 768), BF16)],
        compiler_params=pltpu.CompilerParams(vmem_limit_bytes=20 << 20),
    )(turned, before, *parts)


def silu_slope(hidden):
    sigmoid_value = jax.nn.sigmoid(hidden)
    return sigmoid_value * (1.0 + hidden * (1.0 - sigmoid_value))


def dot(a, b):
    return jnp.dot(a, b, preferred_element_type=F32)


def per_device(features, cotangent, w_self, w_neigh, degree, block_cols, block_count, blocks):
    row, col = lax.axis_index("row"), lax.axis_index("col")
    core, ring, far = col % 2, (col // 2) % RING, col // 16
    offsets = jnp.array(OFFSETS, jnp.int32)
    ring_at = (ring + offsets) % RING
    core_at = jnp.arange(2, dtype=jnp.int32) ^ core
    far_at = jnp.arange(2, dtype=jnp.int32) ^ far
    table = (
        far_at[None, None, :] * 16 + ring_at[None, :, None] * 2 + core_at[:, None, None]
    ).reshape(-1)
    lists = (table, (block_cols[0, 0] ^ row).reshape(-1), block_count[0, 0])
    tile_blocks = blocks[0, 0]
    degree_f = degree.astype(F32)[:, None]
    pieces = [features] + [None] * 7
    for d in (1, 2, 6, 4):
        pieces[d] = to_row(features, d)
    for d in (2, 6, 4):
        pieces[d ^ 1] = to_row(pieces[1], d)
    self_part = dot(features, w_self)
    pieces, self_part = lax.optimization_barrier((pieces, self_part))

    sent = sums(lists, tile_blocks, pieces, 1, 0, 1)
    got = to_partner(sent)
    sent, pieces = lax.optimization_barrier((sent, pieces))
    sent2 = sums(lists, tile_blocks, pieces, 1, 1, 3)
    got2 = to_partner(sent2)
    sent2, pieces = lax.optimization_barrier((sent2, pieces))
    far4 = sums(lists, tile_blocks, pieces, 0, 0, 1, got)
    up, down, pieces = lax.optimization_barrier(
        (far4[:128].astype(BF16), far4[128:].astype(BF16), pieces)
    )
    up, down = along(up, 1), along(down, -1)
    near3 = sums(lists, tile_blocks, pieces, 0, 1, 3, got2)
    near3, pieces = lax.optimization_barrier((near3, pieces))
    sent3 = sums(lists, tile_blocks, pieces, 1, 3, 5)
    got3 = to_partner(sent3)
    up = jnp.concatenate([near3[:128] + up.astype(F32), near3[128:256]], axis=0).astype(BF16)
    down = jnp.concatenate([near3[256:384], near3[384:] + down.astype(F32)], axis=0).astype(BF16)
    up, down, sent3, pieces = lax.optimization_barrier((up, down, sent3, pieces))
    up, down = along(up, 1), along(down, -1)
    sent4 = sums(lists, tile_blocks, pieces, 1, 5, 8)
    got4 = to_partner(sent4)
    sent4, pieces = lax.optimization_barrier((sent4, pieces))
    near2 = sums(lists, tile_blocks, pieces, 0, 3, 5, got3)
    up = (near2[:256] + up.astype(F32)).astype(BF16)
    down = (near2[256:] + down.astype(F32)).astype(BF16)
    up, down, pieces, lists = lax.optimization_barrier((up, down, pieces, lists))
    up, down = along(up, 1), along(down, -1)
    turned_late = turn(lists, tile_blocks, 0, 3)
    near = sums(lists, tile_blocks, pieces, 0, 5, 8, got4)
    up = (near[:256] + up.astype(F32)).astype(BF16)
    down = (near[256:512] + down.astype(F32)).astype(BF16)
    up, down, near, lists, turned_late = lax.optimization_barrier((up, down, near, lists, turned_late))
    up, down = along(up, 1), along(down, -1)
    turned = turn(lists, tile_blocks, 3, 8)
    up, down, turned = lax.optimization_barrier((up, down, turned))
    ends = near[512:] + up.astype(F32) + down.astype(F32)
    summed = ends[:128] + to_far(ends[128:].astype(BF16)).astype(F32)

    aggregate = (summed / degree_f).astype(BF16)
    hidden = self_part + dot(aggregate, w_neigh)
    output = jax.nn.silu(hidden).astype(BF16)
    slope = cotangent.astype(F32) * silu_slope(hidden)
    hidden_grad = slope.astype(BF16)
    shared = (slope / degree_f).astype(BF16)

    across = (((0,), (0,)), ((), ()))
    kept = jnp.where(core == 0, features, aggregate)
    given = jnp.where(core == 0, aggregate, features)
    given = lax.dot_general(given, hidden_grad, across, preferred_element_type=F32).astype(BF16)
    far_shared = to_far(shared)
    pair = lax.dot_general(kept, hidden_grad, across, preferred_element_type=F32)
    shared, given, pair = lax.optimization_barrier(
        (jnp.concatenate([shared, far_shared], axis=0), given, pair)
    )

    held, there = {0: (shared,)}, {}
    given = to_partner(given)
    up, down = along(shared, 1), along(shared, -1)
    up, down, given = lax.optimization_barrier((up, down, given))
    held[7], held[1] = (up,), (down,)
    pair = (pair + given.astype(F32)).astype(BF16)
    part = lax.all_to_all(pair.reshape(ROWS, 96, 768), "row", 0, 0, tiled=True)
    up, down = along(up, 1), along(down, -1)
    held[6], held[2] = (up,), (down,)
    for o in (0, 7, 1, 6, 2):
        there[o] = tuple(to_partner(p) for p in held[o])
    before = spread(turned, [p for o in OFFSETS[3:] for p in held[o] + there[o]])
    up, down = along(up, 1), along(down, -1)
    part = jnp.sum(part.astype(F32), axis=0).astype(BF16)
    part = lax.all_to_all(
        part.reshape(16, 6, 768), "col", 0, 0, axis_index_groups=column_groups(), tiled=True
    )
    up, down, part = lax.optimization_barrier((up, down, part))
    held[5], held[3] = (up,), (down,)
    held[4] = (along(up[:128], 1), along(down[128:], -1))
    for o in (5, 3):
        there[o] = tuple(to_partner(p) for p in held[o])
    held[4], there[5], there[3], before = lax.optimization_barrier(
        (held[4], there[5], there[3], before)
    )
    there[4] = tuple(to_partner(p) for p in held[4])
    chunks = last_spread(turned_late, [p for o in OFFSETS[:3] for p in held[o] + there[o]], before)
    chunks, part = lax.optimization_barrier((chunks, part))

    first = [to_row(chunks[d], d) for d in (2, 6, 1, 4)]
    grad_scale = float(128 * ROWS * COLS) ** (-0.5)
    part = (jnp.sum(part.astype(F32), axis=0) * grad_scale).astype(BF16)
    part = lax.all_to_all(
        jnp.broadcast_to(part[None], (16, 6, 768)), "col", 0, 0, axis_index_groups=column_groups(), tiled=True
    ).reshape(96, 768)
    rest = chunks[3], chunks[5], chunks[7]
    first, rest, part = lax.optimization_barrier((first, rest, part))
    second = [to_row(value, d) for value, d in zip(rest, (3, 5, 7))]
    full = lax.all_to_all(jnp.broadcast_to(part[None], (ROWS, 96, 768)), "row", 0, 0, tiled=True)
    full = full.reshape(768, 768)
    other = to_partner(full)
    grad_w_self = jnp.where(core == 0, full, other).astype(F32)
    grad_w_neigh = jnp.where(core == 0, other, full).astype(F32)
    back = chunks[0]
    for value in first + second:
        back = back + value.astype(F32)
    against = (((1,), (1,)), ((), ()))
    grad_features = (
        lax.dot_general(hidden_grad, w_self, against, preferred_element_type=F32)
        + lax.dot_general(back.astype(BF16), w_neigh, against, preferred_element_type=F32)
    ).astype(BF16)
    return (output, grad_features, grad_w_self, grad_w_neigh)


def solution(mesh):
    placed = (
        P(("row", "col"), None),
        P(("row", "col"), None),
        P(),
        P(),
        P(("row", "col")),
        P("row", "col", None, None),
        P("row", "col", None),
        P("row", "col", None, None, None, None),
    )
    return jax.shard_map(
        per_device,
        mesh=mesh,
        in_specs=placed,
        out_specs=(P(("row", "col"), None), P(("row", "col"), None), P(), P()),
        check_vma=False,
    )
```

```python
import functools

import jax
import jax.numpy as jnp
from jax import lax
from jax.experimental import pallas as pl
from jax.experimental.pallas import tpu as pltpu
from jax.sharding import PartitionSpec as P

ROWS, COLS, RING = 8, 32, 8
OFFSETS = (4, 3, 5, 2, 6, 1, 7, 0)
F32, BF16 = jnp.float32, jnp.bfloat16


def to_partner(value):
    return lax.ppermute(value, "col", [(j, j ^ 1) for j in range(COLS)])


def to_far(value):
    return lax.ppermute(value, "col", [(j, j ^ 16) for j in range(COLS)])


def along(value, step):
    pairs = [(j, (j & 17) | (((j // 2 + step) % RING) * 2)) for j in range(COLS)]
    return lax.ppermute(value, "col", pairs)


def to_row(value, flip):
    return lax.ppermute(value, "row", [(i, i ^ flip) for i in range(ROWS)])


def column_groups():
    return [[c for c in range(COLS) if c % 2 == k] for k in range(2)]


def turn_kernel(lo, table, cols, count, first, second, turned):
    step = pl.program_id(0) + lo * 2
    turned[...] = jnp.zeros_like(turned)
    for part, blocks in enumerate((first, second)):
        row = table[(step % 2) * 16 + (step // 2) * 2 + part]
        for slot in range(4):
            @pl.when(slot < count[row])
            def _():
                at = pl.multiple_of(cols[row * 4 + slot] * 128, 128)
                turned[pl.ds(at, 128), part * 128 : part * 128 + 128] = blocks[0, slot].T


def turn(lists, blocks, lo, hi):
    def spec(part):
        return pl.BlockSpec(
            (1, 4, 128, 128),
            lambda s, t, c, n: (t[(s % 2) * 16 + (s // 2 + lo) * 2 + part], 0, 0, 0),
        )

    return pl.pallas_call(
        functools.partial(turn_kernel, lo),
        out_shape=jax.ShapeDtypeStruct((1024, (hi - lo) * 512), BF16),
        grid_spec=pltpu.PrefetchScalarGridSpec(
            num_scalar_prefetch=3,
            grid=((hi - lo) * 2,),
            in_specs=[spec(0), spec(1)],
            out_specs=pl.BlockSpec((1024, 256), lambda s, t, c, n: (0, s)),
        ),
        compiler_params=pltpu.CompilerParams(vmem_limit_bytes=12 << 20),
    )(*lists, blocks, blocks)


def sums_kernel(start, crossed, table, cols, count, first, second, *refs):
    pieces, rest = refs[:ROWS], refs[ROWS:]
    out, sources, dense = rest[-3:]
    step = pl.program_id(0)

    @pl.when(step == 0)
    def _():
        for d in range(ROWS):
            sources[d * 128 : d * 128 + 128, :] = pieces[d][...]

    dense[...] = jnp.zeros_like(dense)
    for part, blocks in enumerate((first, second)):
        row = table[start + step * 2 + part]
        for slot in range(4):
            @pl.when(slot < count[row])
            def _():
                at = pl.multiple_of(cols[row * 4 + slot] * 128, 128)
                dense[part * 128 : part * 128 + 128, pl.ds(at, 128)] = blocks[0, slot]
    value = jnp.dot(dense[...], sources[...], preferred_element_type=F32)
    if crossed:
        value = value + rest[0][...].astype(F32)
    out[...] = value.astype(out.dtype)


def sums(lists, blocks, pieces, side, lo, hi, crossed=None):
    start = side * 16 + lo * 2

    def spec(part):
        return pl.BlockSpec((1, 4, 128, 128), lambda s, t, c, n: (t[start + s * 2 + part], 0, 0, 0))

    line = pl.BlockSpec((256, 768), lambda s, t, c, n: (s, 0))
    whole = pl.BlockSpec((128, 768), lambda s, t, c, n: (0, 0))
    added = [] if crossed is None else [crossed]
    return pl.pallas_call(
        functools.partial(sums_kernel, start, crossed is not None),
        out_shape=jax.ShapeDtypeStruct(((hi - lo) * 256, 768), BF16 if crossed is None else F32),
        grid_spec=pltpu.PrefetchScalarGridSpec(
            num_scalar_prefetch=3,
            grid=(hi - lo,),
            in_specs=[spec(0), spec(1)] + [whole] * ROWS + [line] * len(added),
            out_specs=line,
            scratch_shapes=[pltpu.VMEM((1024, 768), BF16), pltpu.VMEM((256, 1024), BF16)],
        ),
        compiler_params=pltpu.CompilerParams(vmem_limit_bytes=12 << 20),
    )(*lists, blocks, blocks, *pieces, *added)


VM = pl.BlockSpec(memory_space=pltpu.VMEM)


def stack(parts, held):
    at = 0
    for part in parts:
        held[at : at + part.shape[0], :] = part[...]
        at += part.shape[0]
    return at


def spread_kernel(n, turned, *refs):
    parts, out, held = refs[:n], refs[-2], refs[-1]

    @pl.when(pl.program_id(0) == 0)
    def _():
        stack(parts, held)

    out[...] = jnp.dot(turned[...], held[...], preferred_element_type=F32)


def spread(turned, parts):
    width = sum(p.shape[0] for p in parts)
    return pl.pallas_call(
        functools.partial(spread_kernel, len(parts)),
        out_shape=jax.ShapeDtypeStruct((1024, 768), F32),
        grid=(4,),
        in_specs=[pl.BlockSpec((256, width), lambda d: (d, 0))] + [VM] * len(parts),
        out_specs=pl.BlockSpec((256, 768), lambda d: (d, 0)),
        scratch_shapes=[pltpu.VMEM((width, 768), BF16)],
        compiler_params=pltpu.CompilerParams(vmem_limit_bytes=16 << 20),
    )(turned, *parts)


def last_kernel(n, turned, before, *refs):
    parts, outs, held = refs[:n], refs[n:-1], refs[-1]
    stack(parts, held)
    for d in range(ROWS):
        rows = slice(d * 128, d * 128 + 128)
        value = jnp.dot(turned[rows, :], held[...], preferred_element_type=F32) + before[rows, :]
        outs[d][...] = value.astype(outs[d].dtype)


def last_spread(turned, parts, before):
    width = sum(p.shape[0] for p in parts)
    return pl.pallas_call(
        functools.partial(last_kernel, len(parts)),
        out_shape=[jax.ShapeDtypeStruct((128, 768), BF16 if d else F32) for d in range(ROWS)],
        in_specs=[VM] * (2 + len(parts)),
        out_specs=[VM] * ROWS,
        scratch_shapes=[pltpu.VMEM((width, 768), BF16)],
        compiler_params=pltpu.CompilerParams(vmem_limit_bytes=20 << 20),
    )(turned, before, *parts)


def silu_slope(hidden):
    sigmoid_value = jax.nn.sigmoid(hidden)
    return sigmoid_value * (1.0 + hidden * (1.0 - sigmoid_value))


def dot(a, b):
    return jnp.dot(a, b, preferred_element_type=F32)


def per_device(features, cotangent, w_self, w_neigh, degree, block_cols, block_count, blocks):
    row, col = lax.axis_index("row"), lax.axis_index("col")
    core, ring, far = col % 2, (col // 2) % RING, col // 16
    offsets = jnp.array(OFFSETS, jnp.int32)
    ring_at = (ring + offsets) % RING
    core_at = jnp.arange(2, dtype=jnp.int32) ^ core
    far_at = jnp.arange(2, dtype=jnp.int32) ^ far
    table = (
        far_at[None, None, :] * 16 + ring_at[None, :, None] * 2 + core_at[:, None, None]
    ).reshape(-1)
    lists = (table, (block_cols[0, 0] ^ row).reshape(-1), block_count[0, 0])
    tile_blocks = blocks[0, 0]
    degree_f = degree.astype(F32)[:, None]
    pieces = [features] + [None] * 7
    for d in (1, 2, 6, 4):
        pieces[d] = to_row(features, d)
    for d in (2, 6, 4):
        pieces[d ^ 1] = to_row(pieces[1], d)
    self_part = dot(features, w_self)
    pieces, self_part = lax.optimization_barrier((pieces, self_part))

    sent = sums(lists, tile_blocks, pieces, 1, 0, 1)
    got = to_partner(sent)
    sent, pieces = lax.optimization_barrier((sent, pieces))
    sent2 = sums(lists, tile_blocks, pieces, 1, 1, 3)
    got2 = to_partner(sent2)
    sent2, pieces = lax.optimization_barrier((sent2, pieces))
    far4 = sums(lists, tile_blocks, pieces, 0, 0, 1, got)
    up, down, pieces = lax.optimization_barrier(
        (far4[:128].astype(BF16), far4[128:].astype(BF16), pieces)
    )
    up, down = along(up, 1), along(down, -1)
    near3 = sums(lists, tile_blocks, pieces, 0, 1, 3, got2)
    near3, pieces = lax.optimization_barrier((near3, pieces))
    sent3 = sums(lists, tile_blocks, pieces, 1, 3, 5)
    got3 = to_partner(sent3)
    up = jnp.concatenate([near3[:128] + up.astype(F32), near3[128:256]], axis=0).astype(BF16)
    down = jnp.concatenate([near3[256:384], near3[384:] + down.astype(F32)], axis=0).astype(BF16)
    up, down, sent3, pieces = lax.optimization_barrier((up, down, sent3, pieces))
    up, down = along(up, 1), along(down, -1)
    sent4 = sums(lists, tile_blocks, pieces, 1, 5, 8)
    got4 = to_partner(sent4)
    sent4, pieces = lax.optimization_barrier((sent4, pieces))
    near2 = sums(lists, tile_blocks, pieces, 0, 3, 5, got3)
    up = (near2[:256] + up.astype(F32)).astype(BF16)
    down = (near2[256:] + down.astype(F32)).astype(BF16)
    up, down, pieces, lists = lax.optimization_barrier((up, down, pieces, lists))
    up, down = along(up, 1), along(down, -1)
    turned_late = turn(lists, tile_blocks, 0, 3)
    near = sums(lists, tile_blocks, pieces, 0, 5, 8, got4)
    up = (near[:256] + up.astype(F32)).astype(BF16)
    down = (near[256:512] + down.astype(F32)).astype(BF16)
    up, down, near, lists, turned_late = lax.optimization_barrier((up, down, near, lists, turned_late))
    up, down = along(up, 1), along(down, -1)
    turned = turn(lists, tile_blocks, 3, 8)
    up, down, turned = lax.optimization_barrier((up, down, turned))
    ends = near[512:] + up.astype(F32) + down.astype(F32)
    summed = ends[:128] + to_far(ends[128:].astype(BF16)).astype(F32)

    aggregate = (summed / degree_f).astype(BF16)
    hidden = self_part + dot(aggregate, w_neigh)
    output = jax.nn.silu(hidden).astype(BF16)
    slope = cotangent.astype(F32) * silu_slope(hidden)
    hidden_grad = slope.astype(BF16)
    shared = (slope / degree_f).astype(BF16)

    across = (((0,), (0,)), ((), ()))
    kept = jnp.where(core == 0, features, aggregate)
    given = jnp.where(core == 0, aggregate, features)
    given = lax.dot_general(given, hidden_grad, across, preferred_element_type=F32).astype(BF16)
    far_shared = to_far(shared)
    pair = lax.dot_general(kept, hidden_grad, across, preferred_element_type=F32)
    shared, given, pair = lax.optimization_barrier(
        (jnp.concatenate([shared, far_shared], axis=0), given, pair)
    )

    held, there = {0: (shared,)}, {}
    given = to_partner(given)
    up, down = along(shared, 1), along(shared, -1)
    up, down, given = lax.optimization_barrier((up, down, given))
    held[7], held[1] = (up,), (down,)
    pair = (pair + given.astype(F32)).astype(BF16)
    part = lax.all_to_all(pair.reshape(ROWS, 96, 768), "row", 0, 0, tiled=True)
    up, down = along(up, 1), along(down, -1)
    held[6], held[2] = (up,), (down,)
    for o in (0, 7, 1, 6, 2):
        there[o] = tuple(to_partner(p) for p in held[o])
    before = spread(turned, [p for o in OFFSETS[3:] for p in held[o] + there[o]])
    up, down = along(up, 1), along(down, -1)
    part = jnp.sum(part.astype(F32), axis=0).astype(BF16)
    part = lax.all_to_all(
        part.reshape(16, 6, 768), "col", 0, 0, axis_index_groups=column_groups(), tiled=True
    )
    held[5], held[3] = (up,), (down,)
    held[4] = (along(up[:128], 1), along(down[128:], -1))
    for o in (5, 3):
        there[o] = tuple(to_partner(p) for p in held[o])
    held[4], there[5], there[3], before = lax.optimization_barrier(
        (held[4], there[5], there[3], before)
    )
    there[4] = tuple(to_partner(p) for p in held[4])
    chunks = last_spread(turned_late, [p for o in OFFSETS[:3] for p in held[o] + there[o]], before)
    chunks, part = lax.optimization_barrier((chunks, part))

    first = [to_row(chunks[d], d) for d in (2, 6, 1, 4)]
    grad_scale = float(128 * ROWS * COLS) ** (-0.5)
    part = (jnp.sum(part.astype(F32), axis=0) * grad_scale).astype(BF16)
    part = lax.all_to_all(
        jnp.broadcast_to(part[None], (16, 6, 768)), "col", 0, 0, axis_index_groups=column_groups(), tiled=True
    ).reshape(96, 768)
    rest = chunks[3], chunks[5], chunks[7]
    first, rest, part = lax.optimization_barrier((first, rest, part))
    second = [to_row(value, d) for value, d in zip(rest, (3, 5, 7))]
    full = lax.all_to_all(jnp.broadcast_to(part[None], (ROWS, 96, 768)), "row", 0, 0, tiled=True)
    full = full.reshape(768, 768)
    other = to_partner(full)
    grad_w_self = jnp.where(core == 0, full, other).astype(F32)
    grad_w_neigh = jnp.where(core == 0, other, full).astype(F32)
    back = chunks[0]
    for value in first + second:
        back = back + value.astype(F32)
    against = (((1,), (1,)), ((), ()))
    grad_features = (
        lax.dot_general(hidden_grad, w_self, against, preferred_element_type=F32)
        + lax.dot_general(back.astype(BF16), w_neigh, against, preferred_element_type=F32)
    ).astype(BF16)
    return (output, grad_features, grad_w_self, grad_w_neigh)


def solution(mesh):
    placed = (
        P(("row", "col"), None),
        P(("row", "col"), None),
        P(),
        P(),
        P(("row", "col")),
        P("row", "col", None, None),
        P("row", "col", None),
        P("row", "col", None, None, None, None),
    )
    return jax.shard_map(
        per_device,
        mesh=mesh,
        in_specs=placed,
        out_specs=(P(("row", "col"), None), P(("row", "col"), None), P(), P()),
        check_vma=False,
    )
```
